32 devices in a mesh: fsdp: 32 (over z, y, x, core).
Axes of the slice: x: 2, y: 2, z: 4, core: 2. Of those that a mesh axis runs over, the one named last changes fastest.
Arguments:
- hidden_in: float32 [4096, 960], P('fsdp'), may hold values from -6 to 6
- seq_lens: int32 [32, 8], P('fsdp'), may hold values from 0 to 128, as said below
- attn_gain: float32 [960], replicated, may hold values from 0.5 to 1.5
- w_query: bfloat16 [921600], P('fsdp'), may hold values from -0.1875 to 0.1875
- w_key: bfloat16 [307200], P('fsdp'), may hold values from -0.1875 to 0.1875
- w_value: bfloat16 [307200], P('fsdp'), may hold values from -0.1875 to 0.1875
- w_output: bfloat16 [921600], P('fsdp'), may hold values from -0.5 to 0.5
- mlp_gain: float32 [960], replicated, may hold values from 0.5 to 1.5
- w_gate: bfloat16 [2457600], P('fsdp'), may hold values from -0.1875 to 0.1875
- w_up: bfloat16 [2457600], P('fsdp'), may hold values from -0.1875 to 0.1875
- w_down: bfloat16 [2457600], P('fsdp'), may hold values from -0.125 to 0.125
- grad_out: float32 [4096, 960], P('fsdp'), may hold values from -6 to 6
Outputs:
- hidden_out: float32 [4096, 960], P('fsdp')
- grad_in: float32 [4096, 960], P('fsdp')
- grad_attn_gain: float32 [960], replicated
- grad_mlp_gain: float32 [960], replicated
- grad_query: float32 [921600], P('fsdp')
- grad_key: float32 [307200], P('fsdp')
- grad_value: float32 [307200], P('fsdp')
- grad_output: float32 [921600], P('fsdp')
- grad_gate: float32 [2457600], P('fsdp')
- grad_up: float32 [2457600], P('fsdp')
- grad_down: float32 [2457600], P('fsdp')
The draws below stay inside these ranges and needn't reach their ends.
Inputs may be any that keep to these rules, and one draw needn't show every extreme that they name: `seq_lens`: each device's 8 lengths sum to 128; a length 0 is an empty slot; in every draw some device holds one sequence of 128 tokens.
All inputs are finite; a program needn't handle non-finite values.
Results may differ from the reference program's by a relative error of at most 0.012.
Values may be sent and summed in bfloat16 or wider, within the bound.
No kernel may reach another device: no remote copies, remote signals or barrier semaphores. Data moves between devices by JAX's collectives and lax.ppermute only.
A program may use at most 256 MiB of HBM per device.

```python
import math
import jax
import jax.numpy as jnp
from jax import lax

D = 960
HEADS = 15
KV_HEADS = 5
HEAD_DIM = 64
FF = 2560
TOK_DEV = 128
SLOTS = 8
MAXLEN = 128
NDEV = 32
TOKENS = 4096
N_FSDP = 32


def draw_seq_lens(key, part):
    key_loaded, key_pick, key_border = jax.random.split(jax.random.fold_in(key, 7), 3)
    loaded = jax.random.randint(key_loaded, (NDEV,), 0, 4) == 0
    loaded = loaded | (jnp.arange(NDEV) == jax.random.randint(key_pick, (), 0, NDEV))
    stride = TOK_DEV // SLOTS
    offsets = jax.random.randint(key_border, (NDEV, SLOTS - 1), 0, stride)
    interior = jnp.arange(1, SLOTS, dtype=jnp.int32)[None, :] * stride + offsets
    borders = jnp.concatenate([jnp.zeros((NDEV, 1), jnp.int32), interior.astype(jnp.int32), jnp.full((NDEV, 1), TOK_DEV, jnp.int32)], axis=1)
    spread = borders[:, 1:] - borders[:, :-1]
    loaded_row = jnp.zeros((SLOTS,), jnp.int32).at[0].set(MAXLEN).at[1].set(TOK_DEV - MAXLEN)
    return jnp.where(loaded[:, None], loaded_row[None, :], spread).astype(jnp.int32)


def block_levels(own_key, shape, shards, least, high):
    loudness, own = 1.0, jax.random.fold_in(own_key, 6)
    for axis_at, blocks in shards:
        steps = jnp.exp(jax.random.uniform(jax.random.fold_in(own, axis_at), (blocks,), jnp.float32, least / len(shards), high / len(shards)))
        loudness = loudness * jnp.repeat(steps, shape[axis_at] // blocks).reshape([-1 if axis == axis_at else 1 for axis in range(len(shape))])
    return loudness


def noise(key, shape, width, most, cuts=(), kind=jnp.bfloat16):
    loudness = block_levels(key, shape, cuts, -0.22, 0.18) if cuts else 1.0
    array = jax.random.normal(key, shape, jnp.float32) * width * loudness
    return jnp.minimum(jnp.maximum(array, -most), most).astype(kind)


def setup_inputs(seed: int = 0) -> dict:
    keys = jax.random.split(jax.random.key(seed), 13)
    return {
        "hidden_in": noise(keys[0], (TOKENS, D), 1.0, 6.0, ((0, 32),), jnp.float32),
        "seq_lens": draw_seq_lens(jax.random.fold_in(keys[12], 71), 0),
        "attn_gain": jnp.clip(1.0 + 0.1 * jax.random.normal(keys[2], (D,), jnp.float32), 0.5, 1.5),
        "w_query": noise(keys[3], (D * HEADS * HEAD_DIM,), D ** -0.5, 0.1875, ((0, 32),)),
        "w_key": noise(keys[4], (D * KV_HEADS * HEAD_DIM,), D ** -0.5, 0.1875, ((0, 32),)),
        "w_value": noise(keys[5], (D * KV_HEADS * HEAD_DIM,), D ** -0.5, 0.1875, ((0, 32),)),
        "w_output": noise(keys[6], (HEADS * HEAD_DIM * D,), (D // 8) ** -0.5, 0.5, ((0, 32),)),
        "mlp_gain": jnp.clip(1.0 + 0.1 * jax.random.normal(keys[7], (D,), jnp.float32), 0.5, 1.5),
        "w_gate": noise(keys[8], (D * FF,), D ** -0.5, 0.1875, ((0, 32),)),
        "w_up": noise(keys[9], (D * FF,), D ** -0.5, 0.1875, ((0, 32),)),
        "w_down": noise(keys[10], (FF * D,), FF ** -0.5, 0.125, ((0, 32),)),
        "grad_out": noise(keys[11], (TOKENS, D), 1.0, 6.0, ((0, 32),), jnp.float32),
    }


EPS = 1e-05
ROPE_BASE = 100000.0

def product(left, right):
    return jnp.dot(left, right, preferred_element_type=jnp.float32)

def batched(form, left, right):
    return jnp.einsum(form, left.astype(jnp.float32), right.astype(jnp.float32))

def rms_scale(values):
    inverse = lax.rsqrt(lax.optimization_barrier(jnp.mean(values * values, axis=-1, keepdims=True)) + EPS)
    return (inverse, values * inverse)

def rms_back(grad_normed, normed, inverse):
    return inverse * (grad_normed - normed * lax.optimization_barrier(jnp.mean(grad_normed * normed, axis=-1, keepdims=True)))

def seq_layout(lengths, row_count):
    ends = jnp.cumsum(lengths, axis=1).astype(jnp.int32)
    row_index = jnp.arange(row_count, dtype=jnp.int32)
    after = (row_index[None, :, None] >= ends[:, None, :]).astype(jnp.int32)
    segment = lax.optimization_barrier(jnp.sum(after, axis=2)).astype(jnp.int32)
    starts = lax.optimization_barrier(jnp.sum(after * lengths[:, None, :], axis=2)).astype(jnp.int32)
    return (segment, row_index[None, :] - starts)

def rotary_tables(position):
    half_dim = HEAD_DIM // 2
    freqs = ROPE_BASE ** (-(jnp.arange(half_dim, dtype=jnp.float32) * 2.0) / HEAD_DIM)
    angles = position.astype(jnp.float32)[:, :, None] * freqs[None, None, :]
    return (jnp.cos(angles)[:, :, None, :], jnp.sin(angles)[:, :, None, :])

def rotate(vectors, cosine_table, sine_table):
    half_dim = HEAD_DIM // 2
    first, second = (vectors[..., :half_dim], vectors[..., half_dim:])
    return jnp.concatenate([first * cosine_table - second * sine_table, second * cosine_table + first * sine_table], axis=-1)

def rotate_back(vectors, cosine_table, sine_table):
    half_dim = HEAD_DIM // 2
    first, second = (vectors[..., :half_dim], vectors[..., half_dim:])
    return jnp.concatenate([first * cosine_table + second * sine_table, second * cosine_table - first * sine_table], axis=-1)

def masked_scores(queries, key_rot, key_mask):
    score_scale = 1.0 / math.sqrt(HEAD_DIM)
    scores = batched('gqkrd,gskd->gkrqs', queries, key_rot) * score_scale
    return jnp.where(key_mask[:, None, None, :, :], scores, -1e+30)

def forward_pass(hidden_in, lengths, attn_gain, w_query, w_key, w_value, w_output, mlp_gain, w_gate, w_up, w_down):
    groups = lengths.shape[0]
    row_count = hidden_in.shape[0] // groups
    head_count = w_query.shape[1] // HEAD_DIM
    kv_count = w_key.shape[1] // HEAD_DIM
    repeat = head_count // kv_count
    segment, position = seq_layout(lengths, row_count)
    cosine_table, sine_table = rotary_tables(position)
    causal = jnp.arange(row_count)[:, None] >= jnp.arange(row_count)[None, :]
    key_mask = (segment[:, :, None] == segment[:, None, :]) & causal[None, :, :]
    inverse_one, normed_one = rms_scale(hidden_in)
    normed_in = (normed_one * attn_gain).astype(jnp.bfloat16)
    query_proj = product(normed_in, w_query).reshape(groups, row_count, head_count, HEAD_DIM)
    queries = rotate(query_proj, cosine_table, sine_table).astype(jnp.bfloat16)
    queries = queries.reshape(groups, row_count, kv_count, repeat, HEAD_DIM)
    key_proj = product(normed_in, w_key).reshape(groups, row_count, kv_count, HEAD_DIM)
    key_rot = rotate(key_proj, cosine_table, sine_table).astype(jnp.bfloat16)
    value_proj = product(normed_in, w_value).astype(jnp.bfloat16).reshape(groups, row_count, kv_count, HEAD_DIM)
    scores = masked_scores(queries, key_rot, key_mask)
    row_peak = lax.optimization_barrier(jnp.max(scores, axis=-1, keepdims=True))
    row_total = lax.optimization_barrier(jnp.sum(jnp.exp(scores - row_peak), axis=-1, keepdims=True))
    logsum = row_peak + jnp.log(row_total)
    attn_probs = jnp.exp(scores - logsum).astype(jnp.bfloat16)
    context = batched('gkrqs,gskd->gqkrd', attn_probs, value_proj).astype(jnp.bfloat16)
    context = context.reshape(groups * row_count, head_count * HEAD_DIM)
    mixed = hidden_in + product(context, w_output)
    inverse_two, normed_two = rms_scale(mixed)
    normed_mid = (normed_two * mlp_gain).astype(jnp.bfloat16)
    gate_pre = product(normed_mid, w_gate)
    up_proj = product(normed_mid, w_up)
    gate_sigmoid = jax.nn.sigmoid(gate_pre)
    activated = (gate_pre * gate_sigmoid * up_proj).astype(jnp.bfloat16)
    hidden_out = mixed + product(activated, w_down)
    stored = (inverse_one, normed_one, normed_in, queries, key_rot, value_proj, logsum, context, inverse_two, normed_two, normed_mid, gate_pre, up_proj, activated, key_mask, cosine_table, sine_table)
    return (hidden_out, stored)

def mlp_backward(stored, grad_out, mlp_gain, w_gate, w_up, w_down):
    inverse_two, normed_two, normed_mid, gate_pre, up_proj, activated = stored[8:14]
    grad_low = grad_out.astype(jnp.bfloat16)
    grad_down = product(activated.T, grad_low)
    grad_act = product(grad_low, w_down.T)
    gate_sigmoid = jax.nn.sigmoid(gate_pre)
    grad_gate_pre = (grad_act * up_proj * gate_sigmoid * (1.0 + gate_pre * (1.0 - gate_sigmoid))).astype(jnp.bfloat16)
    grad_up_pre = (grad_act * gate_pre * gate_sigmoid).astype(jnp.bfloat16)
    grad_gate = product(normed_mid.T, grad_gate_pre)
    grad_up = product(normed_mid.T, grad_up_pre)
    grad_mid = product(grad_gate_pre, w_gate.T) + product(grad_up_pre, w_up.T)
    grad_mlp_gain = lax.optimization_barrier(jnp.sum(grad_mid * normed_two, axis=0))
    grad_mixed = grad_out + rms_back(grad_mid * mlp_gain, normed_two, inverse_two)
    return (grad_mixed, grad_mlp_gain, grad_gate, grad_up, grad_down)

def attn_backward(stored, grad_mixed, attn_gain, w_query, w_key, w_value, w_output):
    inverse_one, normed_one, normed_in, queries, key_rot, value_proj, logsum, context = stored[:8]
    key_mask, cosine_table, sine_table = stored[14:17]
    groups, row_count, kv_count, repeat, head_dim = queries.shape
    head_count = kv_count * repeat
    score_scale = 1.0 / math.sqrt(HEAD_DIM)
    grad_low = grad_mixed.astype(jnp.bfloat16)
    grad_output = product(context.T, grad_low)
    grad_context = product(grad_low, w_output.T).astype(jnp.bfloat16)
    grad_context = grad_context.reshape(groups, row_count, kv_count, repeat, HEAD_DIM)
    scores = masked_scores(queries, key_rot, key_mask)
    attn_probs = jnp.exp(scores - logsum)
    probs_low = attn_probs.astype(jnp.bfloat16)
    grad_probs = batched('gqkrd,gskd->gkrqs', grad_context, value_proj)
    context_heads = context.reshape(groups, row_count, kv_count, repeat, HEAD_DIM)
    row_dot = lax.optimization_barrier(jnp.sum(grad_context.astype(jnp.float32) * context_heads.astype(jnp.float32), axis=-1))
    row_dot = jnp.transpose(row_dot, (0, 2, 3, 1))[..., None]
    grad_scores = (attn_probs * (grad_probs - row_dot) * score_scale).astype(jnp.bfloat16)
    grad_values = batched('gkrqs,gqkrd->gskd', probs_low, grad_context).astype(jnp.bfloat16)
    grad_values = grad_values.reshape(groups * row_count, kv_count * HEAD_DIM)
    grad_queries = batched('gkrqs,gskd->gqkrd', grad_scores, key_rot).reshape(groups, row_count, head_count, HEAD_DIM)
    grad_queries = rotate_back(grad_queries, cosine_table, sine_table).astype(jnp.bfloat16)
    grad_queries = grad_queries.reshape(groups * row_count, head_count * HEAD_DIM)
    grad_keys = batched('gkrqs,gqkrd->gskd', grad_scores, queries)
    grad_keys = rotate_back(grad_keys, cosine_table, sine_table).astype(jnp.bfloat16)
    grad_keys = grad_keys.reshape(groups * row_count, kv_count * HEAD_DIM)
    grad_query = product(normed_in.T, grad_queries)
    grad_key = product(normed_in.T, grad_keys)
    grad_value = product(normed_in.T, grad_values)
    grad_normed = product(grad_queries, w_query.T) + product(grad_keys, w_key.T) + product(grad_values, w_value.T)
    grad_attn_gain = lax.optimization_barrier(jnp.sum(grad_normed * normed_one, axis=0))
    grad_in = grad_mixed + rms_back(grad_normed * attn_gain, normed_one, inverse_one)
    return (grad_in, grad_attn_gain, grad_query, grad_key, grad_value, grad_output)

def reference(hidden_in, seq_lens, attn_gain, w_query, w_key, w_value, w_output, mlp_gain, w_gate, w_up, w_down, grad_out):
    query_width = HEADS * HEAD_DIM
    kv_width = KV_HEADS * HEAD_DIM
    mat_query = w_query.reshape(D, query_width)
    mat_key = w_key.reshape(D, kv_width)
    mat_value = w_value.reshape(D, kv_width)
    mat_output = w_output.reshape(query_width, D)
    mat_gate = w_gate.reshape(D, FF)
    mat_up = w_up.reshape(D, FF)
    mat_down = w_down.reshape(FF, D)
    group_size = math.gcd(16, N_FSDP)
    block_count = N_FSDP // group_size
    hidden_blocks = hidden_in.reshape(block_count, group_size * TOK_DEV, D)
    grad_blocks = grad_out.reshape(block_count, group_size * TOK_DEV, D)
    len_blocks = seq_lens.reshape(block_count, group_size, SLOTS)

    def one_block(carry, block):
        block_in, block_lens, block_grad = block
        block_out, stored = forward_pass(block_in, block_lens, attn_gain, mat_query, mat_key, mat_value, mat_output, mlp_gain, mat_gate, mat_up, mat_down)
        grad_mixed, grad_mg, grad_gate, grad_up, grad_down = mlp_backward(stored, block_grad, mlp_gain, mat_gate, mat_up, mat_down)
        grad_in, grad_ag, grad_query, grad_key, grad_value, grad_output = attn_backward(stored, grad_mixed, attn_gain, mat_query, mat_key, mat_value, mat_output)
        terms = (grad_ag, grad_mg, grad_query, grad_key, grad_value, grad_output, grad_gate, grad_up, grad_down)
        carry = tuple((total + term for total, term in zip(carry, terms)))
        return (carry, (block_out, grad_in))
    init = (jnp.zeros((D,), jnp.float32), jnp.zeros((D,), jnp.float32), jnp.zeros((D, query_width), jnp.float32), jnp.zeros((D, kv_width), jnp.float32), jnp.zeros((D, kv_width), jnp.float32), jnp.zeros((query_width, D), jnp.float32), jnp.zeros((D, FF), jnp.float32), jnp.zeros((D, FF), jnp.float32), jnp.zeros((FF, D), jnp.float32))
    sums, (outs_all, grads_all) = lax.scan(one_block, init, (hidden_blocks, len_blocks, grad_blocks))
    return (outs_all.reshape(TOKENS, D), grads_all.reshape(TOKENS, D), sums[0], sums[1], sums[2].reshape(-1), sums[3].reshape(-1), sums[4].reshape(-1), sums[5].reshape(-1), sums[6].reshape(-1), sums[7].reshape(-1), sums[8].reshape(-1))
```

```python
import math

import jax
import jax.numpy as jnp
from jax import lax
from jax.experimental import pallas as pl
from jax.experimental.pallas import tpu as pltpu
from jax.sharding import PartitionSpec as P


D = 960
HEADS = 15
KV_HEADS = 5
HEAD_DIM = 64
FF = 2560


EPS = 1e-05
ROPE_BASE = 100000.0
AXIS = "fsdp"
GROUP = 8
SUBLANES = 16
LANES = 128
LOW = jnp.bfloat16


def product(left, right):
    return jnp.dot(left, right, preferred_element_type=jnp.float32)


def product_t(left, right):
    return lax.dot_general(left, right, (((1,), (1,)), ((), ())), preferred_element_type=jnp.float32)


def t_product(left, right):
    return lax.dot_general(left, right, (((0,), (0,)), ((), ())), preferred_element_type=jnp.float32)


def batched(form, left, right):
    return jnp.einsum(form, left, right, preferred_element_type=jnp.float32)


def rms_scale(values):
    inverse = lax.rsqrt(jnp.mean(values * values, axis=-1, keepdims=True) + EPS)
    return (inverse, values * inverse)


def rms_back(grad_normed, normed, inverse):
    return inverse * (grad_normed - normed * jnp.mean(grad_normed * normed, axis=-1, keepdims=True))


def seq_layout(lengths, row_count):
    ends = jnp.cumsum(lengths, axis=1)
    row_index = jnp.arange(row_count, dtype=jnp.int32)
    after = (row_index[None, :, None] >= ends[:, None, :]).astype(jnp.int32)
    segment = jnp.sum(after, axis=2)
    starts = jnp.sum(after * lengths[:, None, :], axis=2)
    return (segment, row_index[None, :] - starts)


def rotary_tables(position):
    half_dim = HEAD_DIM // 2
    freqs = ROPE_BASE ** (-(jnp.arange(half_dim, dtype=jnp.float32) * 2.0) / HEAD_DIM)
    angles = position.astype(jnp.float32)[:, :, None] * freqs[None, None, :]
    return (jnp.cos(angles)[:, :, None, :], jnp.sin(angles)[:, :, None, :])


def rotate(vectors, cosine_table, sine_table):
    half_dim = HEAD_DIM // 2
    first, second = (vectors[..., :half_dim], vectors[..., half_dim:])
    return jnp.concatenate(
        [first * cosine_table - second * sine_table, second * cosine_table + first * sine_table],
        axis=-1,
    )


def rotate_back(vectors, cosine_table, sine_table):
    return rotate(vectors, cosine_table, -sine_table)


def masked_scores(queries, key_rot, key_mask):
    score_scale = 1.0 / math.sqrt(HEAD_DIM)
    scores = batched("gqkrd,gskd->gkrqs", queries, key_rot) * score_scale
    return jnp.where(key_mask[:, None, None, :, :], scores, -1e30)


def attn_core(qkv, lengths):
    groups = lengths.shape[0]
    rows = qkv.shape[0] // groups
    repeat = HEADS // KV_HEADS
    segment, position = seq_layout(lengths, rows)
    cosine, sine = rotary_tables(position)
    causal = jnp.arange(rows)[:, None] >= jnp.arange(rows)[None, :]
    key_mask = (segment[:, :, None] == segment[:, None, :]) & causal[None, :, :]
    q_width, kv_width = HEADS * HEAD_DIM, KV_HEADS * HEAD_DIM
    query = qkv[:, :q_width].reshape(groups, rows, HEADS, HEAD_DIM)
    key = qkv[:, q_width : q_width + kv_width].reshape(groups, rows, KV_HEADS, HEAD_DIM)
    queries = rotate(query, cosine, sine).astype(LOW).reshape(groups, rows, KV_HEADS, repeat, HEAD_DIM)
    key_rot = rotate(key, cosine, sine).astype(LOW)
    values = qkv[:, q_width + kv_width :].astype(LOW).reshape(groups, rows, KV_HEADS, HEAD_DIM)
    scores = masked_scores(queries, key_rot, key_mask)
    peak = jnp.max(scores, axis=-1, keepdims=True)
    logsum = peak + jnp.log(jnp.sum(jnp.exp(scores - peak), axis=-1, keepdims=True))
    probs = jnp.exp(scores - logsum).astype(LOW)
    context = batched("gkrqs,gskd->gqkrd", probs, values).astype(LOW)
    context = context.reshape(groups * rows, q_width)
    return context, (queries, key_rot, values, logsum, context, key_mask, cosine, sine)


def attn_core_back(stored, grad_context):
    queries, key_rot, values, logsum, context, key_mask, cosine, sine = stored
    groups, rows, kv_count, repeat, _ = queries.shape
    score_scale = 1.0 / math.sqrt(HEAD_DIM)
    grad_context = grad_context.reshape(groups, rows, kv_count, repeat, HEAD_DIM)
    probs = jnp.exp(masked_scores(queries, key_rot, key_mask) - logsum)
    grad_probs = batched("gqkrd,gskd->gkrqs", grad_context, values)
    heads = context.reshape(groups, rows, kv_count, repeat, HEAD_DIM)
    row_dot = jnp.sum(grad_context.astype(jnp.float32) * heads.astype(jnp.float32), axis=-1)
    row_dot = jnp.transpose(row_dot, (0, 2, 3, 1))[..., None]
    grad_scores = (probs * (grad_probs - row_dot) * score_scale).astype(LOW)
    grad_values = batched("gkrqs,gqkrd->gskd", probs.astype(LOW), grad_context).astype(LOW)
    grad_queries = batched("gkrqs,gskd->gqkrd", grad_scores, key_rot)
    grad_queries = grad_queries.reshape(groups, rows, HEADS, HEAD_DIM)
    grad_queries = rotate_back(grad_queries, cosine, sine).astype(LOW)
    grad_keys = batched("gkrqs,gqkrd->gskd", grad_scores, queries)
    grad_keys = rotate_back(grad_keys, cosine, sine).astype(LOW)
    flat = groups * rows
    return jnp.concatenate(
        [grad_queries.reshape(flat, -1), grad_keys.reshape(flat, -1), grad_values.reshape(flat, -1)],
        axis=1,
    )


def sum_all(total, terms):
    for term in terms:
        total = total + term.astype(jnp.float32)
    return total


def place(pieces, spots, shape):
    lead = len(spots[0][0])
    table = jnp.stack([jnp.asarray(v, jnp.int32) for piece in spots for spot in piece for v in spot])
    copies = sum(len(piece) for piece in spots)

    def kernel(table_ref, *refs):
        sources, target, sems = refs[: len(pieces)], refs[len(pieces)], refs[len(pieces) + 1]
        started = []
        for source, piece in zip(sources, spots):
            for row in range(len(piece)):
                base = len(started) * lead
                at = tuple(table_ref[base + k] for k in range(lead))
                copy = pltpu.make_async_copy(source.at[row], target.at[at], sems.at[len(started)])
                copy.start()
                started.append(copy)
        for copy in started:
            copy.wait()

    return pl.pallas_call(
        kernel,
        out_shape=jax.ShapeDtypeStruct(shape, pieces[0].dtype),
        in_specs=[pl.BlockSpec(memory_space=pltpu.SMEM)] + [pl.BlockSpec(memory_space=pltpu.VMEM)] * len(pieces),
        out_specs=pl.BlockSpec(memory_space=pl.ANY),
        scratch_shapes=[pltpu.SemaphoreType.DMA((copies,))],
        name="place",
    )(table, *pieces)


class Links:
    def __init__(self, count):
        self.count = count
        self.planes = count // GROUP
        self.me = lax.axis_index(AXIS)
        self.plane = self.me // GROUP
        self.spot = self.me % GROUP
        self.y = self.spot // 4
        self.x = (self.spot // 2) % 2
        self.core = self.me % 2
        self.quads = [[p * GROUP + 2 * k + c for k in range(4)] for p in range(self.planes) for c in range(2)]
        self.pairs = [[2 * k, 2 * k + 1] for k in range(count // 2)]
        self.groups = [[p * GROUP + k for k in range(GROUP)] for p in range(self.planes)]

    def flip(self, value, bit):
        return lax.ppermute(value, AXIS, [(i, i ^ bit) for i in range(self.count)])

    def shift(self, value, step):
        return lax.ppermute(value, AXIS, [(i, (i + step * GROUP) % self.count) for i in range(self.count)])

    def behind(self, step):
        return (self.plane - step) % self.planes

    def gather_planes(self, block):
        pieces = [block] + [self.shift(block, step) for step in range(1, self.planes)]
        spots = [[(self.behind(step),)] for step in range(self.planes)]
        return place([piece[None] for piece in pieces], spots, (self.planes,) + block.shape)

    def send_planes(self, block_of):
        blocks = [block_of((self.plane + step) % self.planes).astype(LOW) for step in range(1, self.planes)]
        return [self.shift(block, step + 1) for step, block in enumerate(blocks)]

    def scatter_planes(self, block_of):
        return sum_all(block_of(self.plane), self.send_planes(block_of))

    def gather_behind(self, block):
        return jnp.stack([block] + [self.shift(block, step) for step in range(1, self.planes)])

    def gather_rest(self, own):
        half = self.planes // 2
        by_x, by_y = self.flip(own, 2), self.flip(own, 4)
        corner_y, corner_x = self.flip(by_x[:half], 4), self.flip(by_y[half:], 2)
        y, x, core = self.y, self.x, self.core
        pieces, spots = [], []
        for value, first, at_y, at_x in (
            (own, 0, y, x),
            (by_x, 0, y, 1 - x),
            (by_y, 0, 1 - y, x),
            (corner_y, 0, 1 - y, 1 - x),
            (corner_x, half, 1 - y, 1 - x),
        ):
            for side, piece in ((core, value), (1 - core, self.flip(value, 1))):
                pieces.append(piece)
                spots.append([(self.behind(first + k), at_y, at_x, side) for k in range(value.shape[0])])
        whole = place(pieces, spots, (self.planes, 2, 2, 2) + own.shape[1:])
        return whole.reshape(self.count * own.shape[1], own.shape[2])

    def scatter_quad(self, part):
        x, y = self.x, self.y
        corner = [half.astype(LOW) for half in part(1 - y, 1 - x)]
        by_y = self.flip(corner[0], 4).astype(jnp.float32)
        by_x = self.flip(corner[1], 2).astype(jnp.float32)
        to_x, to_y, own = part(y, 1 - x), part(1 - y, x), part(y, x)
        to_x = jnp.stack([to_x[0] + by_y, to_x[1]]).astype(LOW)
        to_y = jnp.stack([to_y[0], to_y[1] + by_x]).astype(LOW)
        from_x, from_y = self.flip(to_x, 2), self.flip(to_y, 4)
        return [
            own[k] + from_x[k].astype(jnp.float32) + from_y[k].astype(jnp.float32) for k in range(2)
        ]

    def split_cores(self, table, axis):
        own = lax.dynamic_index_in_dim(table, self.core, axis, keepdims=False)
        away = lax.dynamic_index_in_dim(table, 1 - self.core, axis, keepdims=False)
        return own, away.astype(LOW)

    def join_cores(self, own, away):
        return own + self.flip(away, 1).astype(jnp.float32)

    def split_rows(self, table):
        depth = table.shape[0] // self.count
        return self.split_cores(table.reshape(self.planes, 2, 2, 2, depth, table.shape[1]), 3)

    def scatter_rows(self, sums):
        half, depth = self.planes // 2, sums[0].shape[3]

        def part(at_y, at_x):
            pieces = []
            for table in sums:
                sizes = (self.planes, 1, 1) + table.shape[3:]
                piece = lax.dynamic_slice(table, (0, at_y, at_x, 0, 0), sizes)
                pieces.append(piece.reshape(2, half, depth, table.shape[-1]))
            joined = jnp.concatenate(pieces, axis=-1)
            return joined[0], joined[1]

        return jnp.concatenate(self.scatter_quad(part), axis=0)

    def gather_quietly(self, block):
        count, width = block.shape
        own = block.reshape(2, count // 2, width)
        by_x, by_y = self.flip(own, 2), self.flip(own, 4)
        corner_y, corner_x = self.flip(by_x[:1], 4), self.flip(by_y[1:], 2)
        y, x, core = self.y, self.x, self.core
        pieces, spots = [], []
        for value, first, at_y, at_x in (
            (own, 0, y, x),
            (by_x, 0, y, 1 - x),
            (by_y, 0, 1 - y, x),
            (corner_y, 0, 1 - y, 1 - x),
            (corner_x, 1, 1 - y, 1 - x),
        ):
            for side, piece in ((core, value), (1 - core, self.flip(value, 1))):
                pieces.append(piece)
                spots.append([(side, at_y, at_x, first + k) for k in range(value.shape[0])])
        whole = place(pieces, spots, (2, 2, 2, 2, count // 2, width))
        return whole.reshape(GROUP * count, width)

    def gather_tokens(self, block):
        quad = lax.all_gather(block, AXIS, axis=0, tiled=True, axis_index_groups=self.quads)
        return lax.all_gather(quad, AXIS, axis=0, tiled=True, axis_index_groups=self.pairs)

    def split_tokens(self, rows):
        return self.split_cores(rows.reshape(2, rows.shape[0] // 2, rows.shape[1]), 0)

    def scatter_tokens(self, own):
        count, width = own.shape[0] // 4, own.shape[1]

        def part(at_y, at_x):
            piece = lax.dynamic_slice(own, ((2 * at_y + at_x) * count, 0), (count, width))
            return piece[:, : width // 2], piece[:, width // 2 :]

        return jnp.concatenate(self.scatter_quad(part), axis=1)

    def swap(self, blocks):
        return lax.all_to_all(
            blocks, AXIS, split_axis=0, concat_axis=0, tiled=True, axis_index_groups=self.groups
        )

    def total(self, values):
        bit = 1
        while bit < self.count:
            values = values + self.flip(values, bit)
            bit = 2 * bit
        return values


def padded(depth):
    return -(-depth // SUBLANES) * SUBLANES


def spread_matrix(count, depth):
    wide = padded(depth)
    row = lax.broadcasted_iota(jnp.int32, (count * depth, count * wide), 0)
    column = lax.broadcasted_iota(jnp.int32, (count * depth, count * wide), 1)
    inside = column % wide
    return ((column // wide * depth + inside == row) & (inside < depth)).astype(LOW)


def pad_rows(block):
    return jnp.pad(block, ((0, padded(block.shape[0]) - block.shape[0]), (0, 0)))


def narrow(values, spread):
    high = lax.reduce_precision(values, 8, 7)
    low = (values - high).astype(LOW)
    return product_t(high.astype(LOW), spread) + product_t(low, spread)


def shards(*args):
    return layer(*args)


def layer(
    hidden_in, seq_lens, attn_gain, w_query, w_key, w_value, w_output, mlp_gain, w_gate, w_up, w_down, grad_out
):
    count = lax.axis_size(AXIS)
    links = Links(count)
    planes = links.planes
    depth, ff_depth = D // count, FF // count
    q_width, kv_width = HEADS * HEAD_DIM, KV_HEADS * HEAD_DIM
    slice_width = planes * ff_depth
    spread = spread_matrix(count, depth)

    qkv_width = q_width + 2 * kv_width
    lanes = -(-qkv_width // LANES) * LANES
    attn_block = jnp.concatenate(
        [
            w_query.reshape(depth, q_width),
            w_key.reshape(depth, kv_width),
            w_value.reshape(depth, kv_width),
            jnp.zeros((depth, lanes - qkv_width), LOW),
            w_output.reshape(depth, D),
        ],
        axis=1,
    )
    pair = jnp.stack([w_gate.reshape(depth, FF), w_up.reshape(depth, FF)])
    pair = pair.reshape(2, depth, planes, GROUP, ff_depth)
    pair = jnp.transpose(pair, (3, 1, 0, 2, 4)).reshape(GROUP, depth, 2 * slice_width)
    pair = links.swap(pair).reshape(GROUP * depth, 2 * slice_width)
    attn_planes = links.gather_behind(pad_rows(attn_block))
    grads = links.gather_quietly(grad_out.astype(LOW))
    attn_planes, w_down = lax.optimization_barrier((attn_planes, w_down))
    attn_table = links.gather_rest(attn_planes)
    attn_table, grads = lax.optimization_barrier((attn_table, grads))
    w_qkv, w_out = attn_table[:, :qkv_width], attn_table[:, lanes:]
    w_pair = links.gather_planes(pair).reshape(D, 2 * slice_width)
    w_back = links.gather_planes(w_down.reshape(ff_depth, D)).reshape(slice_width, D)

    inverse_one, normed_one = rms_scale(hidden_in)
    normed_in = (normed_one * attn_gain).astype(LOW)
    spread_in = product(normed_in, spread).astype(LOW)
    qkv = product(spread_in, w_qkv)
    context, stored = attn_core(qkv, seq_lens)
    spread_context = product(context, spread).astype(LOW)
    mixed = hidden_in + product(spread_context, w_out)

    inverse_two, normed_two = rms_scale(mixed)
    normed_mid = (normed_two * mlp_gain).astype(LOW)
    tokens = links.gather_tokens(normed_mid)
    both = product(tokens, w_pair)
    gate, up = both[:, :slice_width], both[:, slice_width:]
    sigmoid = jax.nn.sigmoid(gate)
    activated = (gate * sigmoid * up).astype(LOW)
    grad_act = product_t(grads, w_back)
    grad_gate = (grad_act * up * sigmoid * (1.0 + gate * (1.0 - sigmoid))).astype(LOW)
    grad_up = (grad_act * gate * sigmoid).astype(LOW)
    grad_both = jnp.concatenate([grad_gate, grad_up], axis=1)
    mid_own, mid_away = links.split_tokens(product_t(grad_both, w_pair))
    mid_away, later_both, later_active = lax.optimization_barrier((mid_away, grad_both, activated))
    pair_term = t_product(tokens, later_both).astype(LOW).reshape(planes, GROUP * depth, 2 * slice_width)
    down_term = t_product(later_active, grads).astype(LOW)
    down_term = down_term.reshape(planes, ff_depth * D // (2 * slice_width), 2 * slice_width)
    ff_term = jnp.concatenate([pair_term, down_term], axis=1)

    def ff_block(p):
        return lax.dynamic_index_in_dim(ff_term, p, 0, keepdims=False)

    ff_own, ff_terms = ff_block(links.plane), links.send_planes(ff_block)
    grad_mid = links.scatter_tokens(links.join_cores(mid_own, mid_away))
    grad_mlp_gain = jnp.sum(grad_mid * normed_two, axis=0)
    grad_mixed = grad_out + rms_back(grad_mid * mlp_gain, normed_two, inverse_two)

    grad_low = grad_mixed.astype(LOW)
    grad_context = product_t(grad_low, w_out).astype(LOW)
    grad_context = product_t(grad_context, spread).astype(LOW)
    grad_qkv = attn_core_back(stored, grad_context)
    own_qkv, away_qkv = links.split_rows(t_product(spread_in, grad_qkv))
    own_out, away_out = links.split_rows(t_product(spread_context, grad_low))

    late = lax.optimization_barrier((away_qkv, away_out, grad_qkv, later_active))
    away_qkv, away_out, late_qkv, late_active = late
    attn_sums = links.scatter_rows([links.join_cores(own_qkv, away_qkv), links.join_cores(own_out, away_out)])
    grad_normed = narrow(product_t(late_qkv, w_qkv), spread)
    grad_attn_gain = jnp.sum(grad_normed * normed_one, axis=0)
    grad_in = grad_mixed + rms_back(grad_normed * attn_gain, normed_one, inverse_one)
    hidden_sums = links.join_cores(*links.split_tokens(product(late_active, w_back)))
    gains = jnp.stack([grad_attn_gain, grad_mlp_gain])
    late = lax.optimization_barrier((attn_sums, hidden_sums, gains, ff_own, ff_terms))
    attn_sums, hidden_sums, gains, ff_own, ff_terms = late
    gains = links.total(gains)
    attn_sum = links.scatter_planes(lambda p: lax.dynamic_index_in_dim(attn_sums, p, 0, keepdims=False))
    attn_sum = attn_sum[:depth]
    qkv_sum, out_sum = attn_sum[:, :qkv_width], attn_sum[:, qkv_width:]
    ff_sum = sum_all(ff_own.astype(jnp.float32), ff_terms)
    pair_sum, down_sum = ff_sum[: GROUP * depth], ff_sum[GROUP * depth :]
    pair_sum = links.swap(pair_sum.astype(LOW).reshape(GROUP, depth, 2 * slice_width)).astype(jnp.float32)
    pair_sum = pair_sum.reshape(GROUP, depth, 2, planes, ff_depth)
    pair_sum = jnp.transpose(pair_sum, (2, 1, 3, 0, 4)).reshape(2, depth * FF)
    hidden_out = mixed + links.scatter_tokens(hidden_sums)
    return (
        hidden_out,
        grad_in,
        gains[0],
        gains[1],
        qkv_sum[:, :q_width].reshape(-1),
        qkv_sum[:, q_width : q_width + kv_width].reshape(-1),
        qkv_sum[:, q_width + kv_width :].reshape(-1),
        out_sum.reshape(-1),
        pair_sum[0],
        pair_sum[1],
        down_sum.reshape(-1),
    )


def forward_pass(
    hidden_in, lengths, attn_gain, w_query, w_key, w_value, w_output, mlp_gain, w_gate, w_up, w_down
):
    groups = lengths.shape[0]
    row_count = hidden_in.shape[0] // groups
    head_count = w_query.shape[1] // HEAD_DIM
    kv_count = w_key.shape[1] // HEAD_DIM
    repeat = head_count // kv_count
    segment, position = seq_layout(lengths, row_count)
    cosine_table, sine_table = rotary_tables(position)
    causal = jnp.arange(row_count)[:, None] >= jnp.arange(row_count)[None, :]
    key_mask = (segment[:, :, None] == segment[:, None, :]) & causal[None, :, :]
    inverse_one, normed_one = rms_scale(hidden_in)
    normed_in = (normed_one * attn_gain).astype(jnp.bfloat16)
    query_proj = product(normed_in, w_query).reshape(groups, row_count, head_count, HEAD_DIM)
    queries = rotate(query_proj, cosine_table, sine_table).astype(jnp.bfloat16)
    queries = queries.reshape(groups, row_count, kv_count, repeat, HEAD_DIM)
    key_proj = product(normed_in, w_key).reshape(groups, row_count, kv_count, HEAD_DIM)
    key_rot = rotate(key_proj, cosine_table, sine_table).astype(jnp.bfloat16)
    value_proj = (
        product(normed_in, w_value)
        .astype(jnp.bfloat16)
        .reshape(groups, row_count, kv_count, HEAD_DIM)
    )
    scores = masked_scores(queries, key_rot, key_mask)
    row_peak = jnp.max(scores, axis=-1, keepdims=True)
    row_total = jnp.sum(jnp.exp(scores - row_peak), axis=-1, keepdims=True)
    logsum = row_peak + jnp.log(row_total)
    attn_probs = jnp.exp(scores - logsum).astype(jnp.bfloat16)
    context = batched("gkrqs,gskd->gqkrd", attn_probs, value_proj).astype(jnp.bfloat16)
    context = context.reshape(groups * row_count, head_count * HEAD_DIM)
    mixed = hidden_in + product(context, w_output)
    inverse_two, normed_two = rms_scale(mixed)
    normed_mid = (normed_two * mlp_gain).astype(jnp.bfloat16)
    gate_pre = product(normed_mid, w_gate)
    up_proj = product(normed_mid, w_up)
    gate_sigmoid = jax.nn.sigmoid(gate_pre)
    activated = (gate_pre * gate_sigmoid * up_proj).astype(jnp.bfloat16)
    hidden_out = mixed + product(activated, w_down)
    stored = (
        inverse_one,
        normed_one,
        normed_in,
        queries,
        key_rot,
        value_proj,
        logsum,
        context,
        inverse_two,
        normed_two,
        normed_mid,
        gate_pre,
        up_proj,
        activated,
        key_mask,
        cosine_table,
        sine_table,
    )
    return (hidden_out, stored)


def mlp_backward(stored, grad_out, mlp_gain, w_gate, w_up, w_down):
    inverse_two, normed_two, normed_mid, gate_pre, up_proj, activated = stored[8:14]
    grad_low = grad_out.astype(jnp.bfloat16)
    grad_act = product(grad_low, w_down.T)
    gate_sigmoid = jax.nn.sigmoid(gate_pre)
    grad_gate_pre = (
        grad_act * up_proj * gate_sigmoid * (1.0 + gate_pre * (1.0 - gate_sigmoid))
    ).astype(jnp.bfloat16)
    grad_up_pre = (grad_act * gate_pre * gate_sigmoid).astype(jnp.bfloat16)
    grad_mid = product(grad_gate_pre, w_gate.T) + product(grad_up_pre, w_up.T)
    grad_mlp_gain = jnp.sum(grad_mid * normed_two, axis=0)
    grad_mixed = grad_out + rms_back(grad_mid * mlp_gain, normed_two, inverse_two)
    pairs = ((normed_mid, grad_gate_pre), (normed_mid, grad_up_pre), (activated, grad_low))
    return (grad_mixed, grad_mlp_gain, pairs)


def attn_backward(stored, grad_mixed, attn_gain, w_query, w_key, w_value, w_output):
    inverse_one, normed_one, normed_in, queries, key_rot, value_proj, logsum, context = stored[:8]
    key_mask, cosine_table, sine_table = stored[14:17]
    groups, row_count, kv_count, repeat, _ = queries.shape
    head_count = kv_count * repeat
    score_scale = 1.0 / math.sqrt(HEAD_DIM)
    grad_low = grad_mixed.astype(jnp.bfloat16)
    grad_context = product(grad_low, w_output.T).astype(jnp.bfloat16)
    grad_context = grad_context.reshape(groups, row_count, kv_count, repeat, HEAD_DIM)
    scores = masked_scores(queries, key_rot, key_mask)
    attn_probs = jnp.exp(scores - logsum)
    probs_low = attn_probs.astype(jnp.bfloat16)
    grad_probs = batched("gqkrd,gskd->gkrqs", grad_context, value_proj)
    context_heads = context.reshape(groups, row_count, kv_count, repeat, HEAD_DIM)
    row_dot = jnp.sum(grad_context.astype(jnp.float32) * context_heads.astype(jnp.float32), axis=-1)
    row_dot = jnp.transpose(row_dot, (0, 2, 3, 1))[..., None]
    grad_scores = (attn_probs * (grad_probs - row_dot) * score_scale).astype(jnp.bfloat16)
    grad_values = batched("gkrqs,gqkrd->gskd", probs_low, grad_context).astype(jnp.bfloat16)
    grad_values = grad_values.reshape(groups * row_count, kv_count * HEAD_DIM)
    grad_queries = batched("gkrqs,gskd->gqkrd", grad_scores, key_rot).reshape(
        groups, row_count, head_count, HEAD_DIM
    )
    grad_queries = rotate_back(grad_queries, cosine_table, sine_table).astype(jnp.bfloat16)
    grad_queries = grad_queries.reshape(groups * row_count, head_count * HEAD_DIM)
    grad_keys = batched("gkrqs,gqkrd->gskd", grad_scores, queries)
    grad_keys = rotate_back(grad_keys, cosine_table, sine_table).astype(jnp.bfloat16)
    grad_keys = grad_keys.reshape(groups * row_count, kv_count * HEAD_DIM)
    grad_normed = (
        product(grad_queries, w_query.T)
        + product(grad_keys, w_key.T)
        + product(grad_values, w_value.T)
    )
    grad_attn_gain = jnp.sum(grad_normed * normed_one, axis=0)
    grad_in = grad_mixed + rms_back(grad_normed * attn_gain, normed_one, inverse_one)
    pairs = (
        (normed_in, grad_queries),
        (normed_in, grad_keys),
        (normed_in, grad_values),
        (context, grad_low),
    )
    return (grad_in, grad_attn_gain, pairs)


def flat_rows(left, right):
    block = lax.dot_general(
        left, right, (((0,), (0,)), ((), ())), preferred_element_type=jnp.float32
    )
    return block.reshape(-1)


def grad_term(pairs, shard_sizes):
    per_device = sum(shard_sizes)

    def term(start, count):
        owners = count // per_device
        pieces = [
            flat_rows(left, right).reshape(owners, size)
            for (left, right), size in zip(pairs, shard_sizes)
        ]
        return jnp.concatenate(pieces, axis=1).reshape(-1)

    return (term, per_device)


def split_shards(summed, shard_sizes):
    pieces = []
    offset = 0
    for size in shard_sizes:
        pieces.append(summed[offset : offset + size])
        offset = offset + size
    return tuple(pieces)


def shape_attn(flat_parts):
    query_width = HEADS * HEAD_DIM
    kv_width = KV_HEADS * HEAD_DIM
    return (
        flat_parts[0].reshape(D, query_width),
        flat_parts[1].reshape(D, kv_width),
        flat_parts[2].reshape(D, kv_width),
        flat_parts[3].reshape(query_width, D),
    )


def shape_mlp(flat_parts):
    return (
        flat_parts[0].reshape(D, FF),
        flat_parts[1].reshape(D, FF),
        flat_parts[2].reshape(FF, D),
    )


def plain_shards(
    hidden_in,
    seq_lens,
    attn_gain,
    w_query,
    w_key,
    w_value,
    w_output,
    mlp_gain,
    w_gate,
    w_up,
    w_down,
    grad_out,
):
    attn_sizes = (w_query.shape[0], w_key.shape[0], w_value.shape[0], w_output.shape[0])
    mlp_sizes = (w_gate.shape[0], w_up.shape[0], w_down.shape[0])
    attn_mats = shape_attn(
        (
            lax.all_gather(w_query, "fsdp", axis=0, tiled=True),
            lax.all_gather(w_key, "fsdp", axis=0, tiled=True),
            lax.all_gather(w_value, "fsdp", axis=0, tiled=True),
            lax.all_gather(w_output, "fsdp", axis=0, tiled=True),
        )
    )
    mlp_mats = shape_mlp(
        (
            lax.all_gather(w_gate, "fsdp", axis=0, tiled=True),
            lax.all_gather(w_up, "fsdp", axis=0, tiled=True),
            lax.all_gather(w_down, "fsdp", axis=0, tiled=True),
        )
    )
    hidden_out, stored = forward_pass(
        hidden_in,
        seq_lens,
        attn_gain,
        attn_mats[0],
        attn_mats[1],
        attn_mats[2],
        attn_mats[3],
        mlp_gain,
        mlp_mats[0],
        mlp_mats[1],
        mlp_mats[2],
    )
    mlp_back = shape_mlp(
        (
            lax.all_gather(w_gate, "fsdp", axis=0, tiled=True),
            lax.all_gather(w_up, "fsdp", axis=0, tiled=True),
            lax.all_gather(w_down, "fsdp", axis=0, tiled=True),
        )
    )
    grad_mixed, grad_mg, mlp_pairs = mlp_backward(
        stored, grad_out, mlp_gain, mlp_back[0], mlp_back[1], mlp_back[2]
    )
    mlp_fn, mlp_rows = grad_term(mlp_pairs, mlp_sizes)
    mlp_shards = split_shards(
        lax.psum_scatter(
            mlp_fn(jnp.int32(0), lax.axis_size("fsdp") * mlp_rows),
            "fsdp",
            scatter_dimension=0,
            tiled=True,
        ),
        mlp_sizes,
    )
    attn_back = shape_attn(
        (
            lax.all_gather(w_query, "fsdp", axis=0, tiled=True),
            lax.all_gather(w_key, "fsdp", axis=0, tiled=True),
            lax.all_gather(w_value, "fsdp", axis=0, tiled=True),
            lax.all_gather(w_output, "fsdp", axis=0, tiled=True),
        )
    )
    grad_in, grad_ag, attn_pairs = attn_backward(
        stored, grad_mixed, attn_gain, attn_back[0], attn_back[1], attn_back[2], attn_back[3]
    )
    attn_fn, attn_rows = grad_term(attn_pairs, attn_sizes)
    attn_shards = split_shards(
        lax.psum_scatter(
            attn_fn(jnp.int32(0), lax.axis_size("fsdp") * attn_rows),
            "fsdp",
            scatter_dimension=0,
            tiled=True,
        ),
        attn_sizes,
    )
    weight_shards = attn_shards + mlp_shards
    gain_totals = lax.psum((grad_ag, grad_mg), "fsdp")
    return (
        hidden_out,
        grad_in,
        gain_totals[0],
        gain_totals[1],
        weight_shards[0],
        weight_shards[1],
        weight_shards[2],
        weight_shards[3],
        weight_shards[4],
        weight_shards[5],
        weight_shards[6],
    )


def solution(mesh):
    placed = (
        P("fsdp", None),
        P("fsdp", None),
        P(),
        P("fsdp"),
        P("fsdp"),
        P("fsdp"),
        P("fsdp"),
        P(),
        P("fsdp"),
        P("fsdp"),
        P("fsdp"),
        P("fsdp", None),
    )
    count = mesh.shape[AXIS]
    whole_rows = D % count == 0 and FF % count == 0 and count in (2 * GROUP, 4 * GROUP)
    return jax.shard_map(
        shards if whole_rows else plain_shards,
        mesh=mesh,
        in_specs=placed,
        out_specs=(
            P("fsdp", None),
            P("fsdp", None),
            P(),
            P(),
            P("fsdp"),
            P("fsdp"),
            P("fsdp"),
            P("fsdp"),
            P("fsdp"),
            P("fsdp"),
            P("fsdp"),
        ),
        check_vma=False,
    )
```

```python
import math

import jax
import jax.numpy as jnp
from jax import lax
from jax.experimental import pallas as pl
from jax.experimental.pallas import tpu as pltpu
from jax.sharding import PartitionSpec as P


D = 960
HEADS = 15
KV_HEADS = 5
HEAD_DIM = 64
FF = 2560


EPS = 1e-05
ROPE_BASE = 100000.0
AXIS = "fsdp"
GROUP = 8
SUBLANES = 16
LANES = 128
LOW = jnp.bfloat16


def product(left, right):
    return jnp.dot(left, right, preferred_element_type=jnp.float32)


def product_t(left, right):
    return lax.dot_general(left, right, (((1,), (1,)), ((), ())), preferred_element_type=jnp.float32)


def t_product(left, right):
    return lax.dot_general(left, right, (((0,), (0,)), ((), ())), preferred_element_type=jnp.float32)


def batched(form, left, right):
    return jnp.einsum(form, left, right, preferred_element_type=jnp.float32)


def rms_scale(values):
    inverse = lax.rsqrt(jnp.mean(values * values, axis=-1, keepdims=True) + EPS)
    return (inverse, values * inverse)


def rms_back(grad_normed, normed, inverse):
    return inverse * (grad_normed - normed * jnp.mean(grad_normed * normed, axis=-1, keepdims=True))


def seq_layout(lengths, row_count):
    ends = jnp.cumsum(lengths, axis=1)
    row_index = jnp.arange(row_count, dtype=jnp.int32)
    after = (row_index[None, :, None] >= ends[:, None, :]).astype(jnp.int32)
    segment = jnp.sum(after, axis=2)
    starts = jnp.sum(after * lengths[:, None, :], axis=2)
    return (segment, row_index[None, :] - starts)


def rotary_tables(position):
    half_dim = HEAD_DIM // 2
    freqs = ROPE_BASE ** (-(jnp.arange(half_dim, dtype=jnp.float32) * 2.0) / HEAD_DIM)
    angles = position.astype(jnp.float32)[:, :, None] * freqs[None, None, :]
    return (jnp.cos(angles)[:, :, None, :], jnp.sin(angles)[:, :, None, :])


def rotate(vectors, cosine_table, sine_table):
    half_dim = HEAD_DIM // 2
    first, second = (vectors[..., :half_dim], vectors[..., half_dim:])
    return jnp.concatenate(
        [first * cosine_table - second * sine_table, second * cosine_table + first * sine_table],
        axis=-1,
    )


def rotate_back(vectors, cosine_table, sine_table):
    return rotate(vectors, cosine_table, -sine_table)


def masked_scores(queries, key_rot, key_mask):
    score_scale = 1.0 / math.sqrt(HEAD_DIM)
    scores = batched("gqkrd,gskd->gkrqs", queries, key_rot) * score_scale
    return jnp.where(key_mask[:, None, None, :, :], scores, -1e30)


def attn_core(qkv, lengths):
    groups = lengths.shape[0]
    rows = qkv.shape[0] // groups
    repeat = HEADS // KV_HEADS
    segment, position = seq_layout(lengths, rows)
    cosine, sine = rotary_tables(position)
    causal = jnp.arange(rows)[:, None] >= jnp.arange(rows)[None, :]
    key_mask = (segment[:, :, None] == segment[:, None, :]) & causal[None, :, :]
    q_width, kv_width = HEADS * HEAD_DIM, KV_HEADS * HEAD_DIM
    query = qkv[:, :q_width].reshape(groups, rows, HEADS, HEAD_DIM)
    key = qkv[:, q_width : q_width + kv_width].reshape(groups, rows, KV_HEADS, HEAD_DIM)
    queries = rotate(query, cosine, sine).astype(LOW).reshape(groups, rows, KV_HEADS, repeat, HEAD_DIM)
    key_rot = rotate(key, cosine, sine).astype(LOW)
    values = qkv[:, q_width + kv_width :].astype(LOW).reshape(groups, rows, KV_HEADS, HEAD_DIM)
    scores = masked_scores(queries, key_rot, key_mask)
    peak = jnp.max(scores, axis=-1, keepdims=True)
    logsum = peak + jnp.log(jnp.sum(jnp.exp(scores - peak), axis=-1, keepdims=True))
    probs = jnp.exp(scores - logsum).astype(LOW)
    context = batched("gkrqs,gskd->gqkrd", probs, values).astype(LOW)
    context = context.reshape(groups * rows, q_width)
    return context, (queries, key_rot, values, logsum, context, key_mask, cosine, sine)


def attn_core_back(stored, grad_context):
    queries, key_rot, values, logsum, context, key_mask, cosine, sine = stored
    groups, rows, kv_count, repeat, _ = queries.shape
    score_scale = 1.0 / math.sqrt(HEAD_DIM)
    grad_context = grad_context.reshape(groups, rows, kv_count, repeat, HEAD_DIM)
    probs = jnp.exp(masked_scores(queries, key_rot, key_mask) - logsum)
    grad_probs = batched("gqkrd,gskd->gkrqs", grad_context, values)
    heads = context.reshape(groups, rows, kv_count, repeat, HEAD_DIM)
    row_dot = jnp.sum(grad_context.astype(jnp.float32) * heads.astype(jnp.float32), axis=-1)
    row_dot = jnp.transpose(row_dot, (0, 2, 3, 1))[..., None]
    grad_scores = (probs * (grad_probs - row_dot) * score_scale).astype(LOW)
    grad_values = batched("gkrqs,gqkrd->gskd", probs.astype(LOW), grad_context).astype(LOW)
    grad_queries = batched("gkrqs,gskd->gqkrd", grad_scores, key_rot)
    grad_queries = grad_queries.reshape(groups, rows, HEADS, HEAD_DIM)
    grad_queries = rotate_back(grad_queries, cosine, sine).astype(LOW)
    grad_keys = batched("gkrqs,gqkrd->gskd", grad_scores, queries)
    grad_keys = rotate_back(grad_keys, cosine, sine).astype(LOW)
    flat = groups * rows
    return jnp.concatenate(
        [grad_queries.reshape(flat, -1), grad_keys.reshape(flat, -1), grad_values.reshape(flat, -1)],
        axis=1,
    )


def sum_all(total, terms):
    for term in terms:
        total = total + term.astype(jnp.float32)
    return total


def place(pieces, spots, shape):
    lead = len(spots[0][0])
    table = jnp.stack([jnp.asarray(v, jnp.int32) for piece in spots for spot in piece for v in spot])
    copies = sum(len(piece) for piece in spots)

    def kernel(table_ref, *refs):
        sources, target, sems = refs[: len(pieces)], refs[len(pieces)], refs[len(pieces) + 1]
        started = []
        for source, piece in zip(sources, spots):
            for row in range(len(piece)):
                base = len(started) * lead
                at = tuple(table_ref[base + k] for k in range(lead))
                copy = pltpu.make_async_copy(source.at[row], target.at[at], sems.at[len(started)])
                copy.start()
                started.append(copy)
        for copy in started:
            copy.wait()

    return pl.pallas_call(
        kernel,
        out_shape=jax.ShapeDtypeStruct(shape, pieces[0].dtype),
        in_specs=[pl.BlockSpec(memory_space=pltpu.SMEM)] + [pl.BlockSpec(memory_space=pltpu.VMEM)] * len(pieces),
        out_specs=pl.BlockSpec(memory_space=pl.ANY),
        scratch_shapes=[pltpu.SemaphoreType.DMA((copies,))],
        name="place",
    )(table, *pieces)


def weight_terms(pairs, starts, width, dtype):
    rows = pairs[0][0].shape[1]

    def kernel(*refs):
        target = refs[-1]
        for k, start in enumerate(starts):
            left, right = refs[2 * k][...], refs[2 * k + 1][...]
            stop = start + right.shape[0]
            term = lax.dot_general(left, right, (((0,), (1,)), ((), ())), preferred_element_type=jnp.float32)
            target[:, start:stop] = term.astype(dtype)
            gap = (starts + [width])[k + 1] - stop
            if gap:
                target[:, stop : stop + gap] = jnp.zeros((rows, gap), dtype)

    here = pl.BlockSpec(memory_space=pltpu.VMEM)
    return pl.pallas_call(
        kernel,
        out_shape=jax.ShapeDtypeStruct((rows, width), dtype),
        in_specs=[here] * (2 * len(pairs)),
        out_specs=here,
        name="weight_terms",
    )(*[array for pair in pairs for array in pair])


class Links:
    def __init__(self, count):
        self.count = count
        self.planes = count // GROUP
        self.me = lax.axis_index(AXIS)
        self.plane = self.me // GROUP
        self.quads = [[p * GROUP + 2 * k + c for k in range(4)] for p in range(self.planes) for c in range(2)]
        self.groups = [[p * GROUP + k for k in range(GROUP)] for p in range(self.planes)]

    def flip(self, value, bit):
        return lax.ppermute(value, AXIS, [(i, i ^ bit) for i in range(self.count)])

    def shift(self, value, step):
        return lax.ppermute(value, AXIS, [(i, (i + step * GROUP) % self.count) for i in range(self.count)])

    def behind(self, step):
        return (self.plane - step) % self.planes

    def device_at(self, place_index):
        step = place_index % self.planes
        chip = place_index // self.planes % 4
        bits = chip % 2 * 2 + chip // 2 * 4 + place_index // (4 * self.planes)
        spot = self.me % GROUP
        flipped = jnp.where(bits & 1, spot ^ 1, spot)
        flipped = jnp.where(bits & 2, flipped ^ 2, flipped)
        flipped = jnp.where(bits & 4, flipped ^ 4, flipped)
        return (self.plane - step) % self.planes * GROUP + flipped

    def gather_planes(self, block):
        pieces = [block] + [self.shift(block, step) for step in range(1, self.planes)]
        spots = [[(self.behind(step),)] for step in range(self.planes)]
        return place([piece[None] for piece in pieces], spots, (self.planes,) + block.shape)

    def send_planes(self, block_of):
        blocks = [block_of((self.plane + step) % self.planes).astype(LOW) for step in range(1, self.planes)]
        return [self.shift(block, step + 1) for step, block in enumerate(blocks)]

    def gather_behind(self, block):
        return jnp.stack([block] + [self.shift(block, step) for step in range(1, self.planes)])

    def scatter_behind(self, rows, late):
        blocks = [rows[step].astype(LOW) for step in range(1, self.planes)]
        blocks, late = lax.optimization_barrier((blocks, late))
        terms = [self.shift(block, -1 - step) for step, block in enumerate(blocks)]
        return sum_all(rows[0], terms), late

    def gather_rows(self, own):
        half = self.planes // 2
        by_x, by_y = self.flip(own, 2), self.flip(own, 4)
        pieces = [own, by_x, by_y, self.flip(by_x[:half], 4), self.flip(by_y[half:], 2)]
        others = [self.flip(piece, 1) for piece in pieces]
        rows = (4 * self.planes * own.shape[1], own.shape[2])
        return jnp.concatenate(pieces).reshape(rows), jnp.concatenate(others).reshape(rows)

    def scatter_quad(self, part, early=(), late=()):
        corner = [part(3, half).astype(LOW) for half in range(2)]
        corner, early = lax.optimization_barrier((corner, early))
        by_y, by_x = self.flip(corner[0], 4), self.flip(corner[1], 2)
        by_y, by_x = by_y.astype(jnp.float32), by_x.astype(jnp.float32)
        to_x = jnp.stack([(part(1, 0) + by_y).astype(LOW), part(1, 1).astype(LOW)])
        to_y = jnp.stack([part(2, 0).astype(LOW), (part(2, 1) + by_x).astype(LOW)])
        to_x, to_y, late = lax.optimization_barrier((to_x, to_y, late))
        from_x, from_y = self.flip(to_x, 2), self.flip(to_y, 4)
        return [sum_all(part(0, half), [from_x[half], from_y[half]]) for half in range(2)], early, late

    def join_cores(self, own, away):
        return own + self.flip(away, 1).astype(jnp.float32)

    def blocks(self, rows):
        return rows.reshape(4 * self.planes, rows.shape[0] // (4 * self.planes), rows.shape[1])

    def scatter_rows(self, table, early, late):
        half = self.planes // 2

        def part(chip, side):
            start = (2 * chip + side) * half
            return table[start : start + half]

        halves, early, late = self.scatter_quad(part, early, late)
        return jnp.concatenate(halves), early, late

    def gather_tokens(self, block):
        quad = lax.all_gather(block, AXIS, axis=0, tiled=True, axis_index_groups=self.quads)
        return quad, self.flip(quad, 1)

    def scatter_tokens(self, own, early=()):
        count, width, spot = own.shape[0] // 4, own.shape[1] // 2, self.me % GROUP // 2

        def part(chip, side):
            return lax.dynamic_slice(own, ((spot ^ chip) * count, side * width), (count, width))

        halves, early, _ = self.scatter_quad(part, early)
        return jnp.concatenate(halves, axis=1), early

    def swap(self, blocks):
        return lax.all_to_all(
            blocks, AXIS, split_axis=0, concat_axis=0, tiled=True, axis_index_groups=self.groups
        )

    def add_over(self, values, bits):
        for bit in bits:
            values = values + self.flip(values, bit)
        return values


def padded(depth):
    return -(-depth // SUBLANES) * SUBLANES


def spread_matrix(links, depth):
    wide = padded(depth)
    column = lax.broadcasted_iota(jnp.int32, (1, links.count * wide), 1)
    inside = column % wide
    source = jnp.where(inside < depth, links.device_at(column // wide) * depth + inside, -1)
    row = lax.broadcasted_iota(jnp.int32, (links.count * depth, links.count * wide), 0)
    return (row == source).astype(LOW)


def pad_rows(block):
    return jnp.pad(block, ((0, padded(block.shape[0]) - block.shape[0]), (0, 0)))


def narrow(values, spread):
    high = lax.reduce_precision(values, 8, 7)
    low = (values - high).astype(LOW)
    return product_t(high.astype(LOW), spread) + product_t(low, spread)


def shards(*args):
    return layer(*args)


def layer(
    hidden_in, seq_lens, attn_gain, w_query, w_key, w_value, w_output, mlp_gain, w_gate, w_up, w_down, grad_out
):
    count = lax.axis_size(AXIS)
    links = Links(count)
    planes = links.planes
    depth, ff_depth = D // count, FF // count
    q_width, kv_width = HEADS * HEAD_DIM, KV_HEADS * HEAD_DIM
    slice_width = planes * ff_depth
    spread = spread_matrix(links, depth)

    qkv_width = q_width + 2 * kv_width
    lanes = -(-qkv_width // LANES) * LANES
    attn_block = jnp.concatenate(
        [
            w_query.reshape(depth, q_width),
            w_key.reshape(depth, kv_width),
            w_value.reshape(depth, kv_width),
            jnp.zeros((depth, lanes - qkv_width), LOW),
            w_output.reshape(depth, D),
        ],
        axis=1,
    )
    attn_planes = links.gather_behind(pad_rows(attn_block))
    grads = links.gather_tokens(grad_out.astype(LOW))
    attn_planes, w_gate, w_up, w_down = lax.optimization_barrier((attn_planes, w_gate, w_up, w_down))
    tables = links.gather_rows(attn_planes)
    pair = jnp.stack([w_gate.reshape(depth, FF), w_up.reshape(depth, FF)])
    pair = pair.reshape(2, depth, planes, GROUP, ff_depth)
    pair = jnp.transpose(pair, (3, 1, 0, 2, 4)).reshape(GROUP, depth, 2 * slice_width)
    pair = links.swap(pair).reshape(GROUP * depth, 2 * slice_width)
    tables, grads = lax.optimization_barrier((tables, grads))
    w_qkv = [table[:, :qkv_width] for table in tables]
    w_out = [table[:, lanes:] for table in tables]
    mine = tables[0].shape[0]
    thirds = jnp.concatenate(jnp.split(w_down.reshape(ff_depth, D), 3, axis=1))
    ff_table = links.gather_planes(jnp.concatenate([pair, thirds], axis=1))

    inverse_one, normed_one = rms_scale(hidden_in)
    normed_in = (normed_one * attn_gain).astype(LOW)
    spread_in = product(normed_in, spread).astype(LOW)
    qkv = product(spread_in[:, :mine], w_qkv[0]) + product(spread_in[:, mine:], w_qkv[1])
    context, stored = attn_core(qkv, seq_lens)
    spread_context = product(context, spread).astype(LOW)
    mixed = hidden_in + (
        product(spread_context[:, :mine], w_out[0]) + product(spread_context[:, mine:], w_out[1])
    )

    inverse_two, normed_two = rms_scale(mixed)
    normed_mid = (normed_two * mlp_gain).astype(LOW)
    w_pair = ff_table[:, :, : 2 * slice_width].reshape(D, 2 * slice_width)
    w_back = jnp.split(ff_table[:, :, 2 * slice_width :], 3, axis=1)
    w_back = jnp.concatenate(w_back, axis=2).reshape(slice_width, D)
    tokens = links.gather_tokens(normed_mid)

    def unit(tokens, grads):
        both = product(tokens, w_pair)
        gate, up = both[:, :slice_width], both[:, slice_width:]
        sigmoid = jax.nn.sigmoid(gate)
        activated = (gate * sigmoid * up).astype(LOW)
        grad_act = product_t(grads, w_back)
        grad_gate = (grad_act * up * sigmoid * (1.0 + gate * (1.0 - sigmoid))).astype(LOW)
        grad_up = (grad_act * gate * sigmoid).astype(LOW)
        grad_both = jnp.concatenate([grad_gate, grad_up], axis=1)
        return activated, grad_both, product_t(grad_both, w_pair)

    far_active, far_both, mid_away = unit(tokens[1], grads[1])
    near_active, near_both, mid_own = unit(tokens[0], grads[0])
    grad_mid, early = links.scatter_tokens(
        links.join_cores(mid_own, mid_away.astype(LOW)), (near_both, far_both, near_active, far_active)
    )
    near_both, far_both, near_active, far_active = early
    pair_term = (t_product(tokens[0], near_both) + t_product(tokens[1], far_both)).astype(LOW)
    pair_term = pair_term.reshape(planes, GROUP * depth, 2 * slice_width)
    down_term = (t_product(near_active, grads[0]) + t_product(far_active, grads[1])).astype(LOW)
    down_term = down_term.reshape(planes, ff_depth, D)

    def ff_block(p):
        down = lax.dynamic_index_in_dim(down_term, p, 0, keepdims=False)
        thirds = jnp.concatenate(jnp.split(down, 3, axis=1))
        return jnp.concatenate([lax.dynamic_index_in_dim(pair_term, p, 0, keepdims=False), thirds], axis=1)

    ff_own, ff_terms = ff_block(links.plane), links.send_planes(ff_block)
    grad_mlp_gain = jnp.sum(grad_mid * normed_two, axis=0)
    grad_mixed = grad_out + rms_back(grad_mid * mlp_gain, normed_two, inverse_two)

    grad_low = grad_mixed.astype(LOW)
    grad_context = jnp.concatenate([product_t(grad_low, part).astype(LOW) for part in w_out], axis=1)
    grad_context = product_t(grad_context, spread).astype(LOW)
    grad_qkv = attn_core_back(stored, grad_context)
    far_term, near_term = [
        weight_terms(
            [(spread_in[:, side], grad_qkv.T), (spread_context[:, side], grad_low.T)],
            [0, lanes],
            lanes + D,
            dtype,
        )
        for side, dtype in ((slice(mine, None), LOW), (slice(0, mine), jnp.float32))
    ]
    attn_sums = links.join_cores(links.blocks(near_term), links.blocks(far_term))

    late = (near_active, far_active, ff_own, ff_terms)
    attn_sums, late_qkv, late = links.scatter_rows(attn_sums, grad_qkv, late)
    near_active, far_active, ff_own, ff_terms = late
    grad_normed = jnp.concatenate([product_t(late_qkv, part) for part in w_qkv], axis=1)
    grad_normed = narrow(grad_normed, spread)
    grad_attn_gain = jnp.sum(grad_normed * normed_one, axis=0)
    grad_in = grad_mixed + rms_back(grad_normed * attn_gain, normed_one, inverse_one)
    plane_bits = [GROUP << k for k in range(planes.bit_length() - 1)]
    gains = links.add_over(jnp.stack([grad_attn_gain, grad_mlp_gain]), plane_bits + [1])
    hidden_sums = links.join_cores(product(near_active, w_back), product(far_active, w_back).astype(LOW))
    ff_sum = sum_all(ff_own.astype(jnp.float32), ff_terms)
    pair_sum, down_sum = ff_sum[:, : 2 * slice_width], ff_sum[:, 2 * slice_width :]
    down_sum = jnp.concatenate(jnp.split(down_sum, 3), axis=1)
    pair_sum = pair_sum.astype(LOW).reshape(GROUP, depth, 2 * slice_width)
    attn_sum, late = links.scatter_behind(attn_sums, (hidden_sums, pair_sum, gains))
    hidden_sums, pair_sum, gains = late
    gains = links.add_over(gains, [2, 4])
    attn_sum = attn_sum[:depth]
    qkv_sum, out_sum = attn_sum[:, :qkv_width], attn_sum[:, lanes:]
    pair_sum = links.swap(pair_sum)
    pair_sum = pair_sum.astype(jnp.float32).reshape(GROUP, depth, 2, planes, ff_depth)
    pair_sum = jnp.transpose(pair_sum, (2, 1, 3, 0, 4)).reshape(2, depth * FF)
    hidden_out = mixed + links.scatter_tokens(hidden_sums)[0]
    return (
        hidden_out,
        grad_in,
        gains[0],
        gains[1],
        qkv_sum[:, :q_width].reshape(-1),
        qkv_sum[:, q_width : q_width + kv_width].reshape(-1),
        qkv_sum[:, q_width + kv_width :].reshape(-1),
        out_sum.reshape(-1),
        pair_sum[0],
        pair_sum[1],
        down_sum.reshape(-1),
    )


def forward_pass(
    hidden_in, lengths, attn_gain, w_query, w_key, w_value, w_output, mlp_gain, w_gate, w_up, w_down
):
    groups = lengths.shape[0]
    row_count = hidden_in.shape[0] // groups
    head_count = w_query.shape[1] // HEAD_DIM
    kv_count = w_key.shape[1] // HEAD_DIM
    repeat = head_count // kv_count
    segment, position = seq_layout(lengths, row_count)
    cosine_table, sine_table = rotary_tables(position)
    causal = jnp.arange(row_count)[:, None] >= jnp.arange(row_count)[None, :]
    key_mask = (segment[:, :, None] == segment[:, None, :]) & causal[None, :, :]
    inverse_one, normed_one = rms_scale(hidden_in)
    normed_in = (normed_one * attn_gain).astype(jnp.bfloat16)
    query_proj = product(normed_in, w_query).reshape(groups, row_count, head_count, HEAD_DIM)
    queries = rotate(query_proj, cosine_table, sine_table).astype(jnp.bfloat16)
    queries = queries.reshape(groups, row_count, kv_count, repeat, HEAD_DIM)
    key_proj = product(normed_in, w_key).reshape(groups, row_count, kv_count, HEAD_DIM)
    key_rot = rotate(key_proj, cosine_table, sine_table).astype(jnp.bfloat16)
    value_proj = (
        product(normed_in, w_value)
        .astype(jnp.bfloat16)
        .reshape(groups, row_count, kv_count, HEAD_DIM)
    )
    scores = masked_scores(queries, key_rot, key_mask)
    row_peak = jnp.max(scores, axis=-1, keepdims=True)
    row_total = jnp.sum(jnp.exp(scores - row_peak), axis=-1, keepdims=True)
    logsum = row_peak + jnp.log(row_total)
    attn_probs = jnp.exp(scores - logsum).astype(jnp.bfloat16)
    context = batched("gkrqs,gskd->gqkrd", attn_probs, value_proj).astype(jnp.bfloat16)
    context = context.reshape(groups * row_count, head_count * HEAD_DIM)
    mixed = hidden_in + product(context, w_output)
    inverse_two, normed_two = rms_scale(mixed)
    normed_mid = (normed_two * mlp_gain).astype(jnp.bfloat16)
    gate_pre = product(normed_mid, w_gate)
    up_proj = product(normed_mid, w_up)
    gate_sigmoid = jax.nn.sigmoid(gate_pre)
    activated = (gate_pre * gate_sigmoid * up_proj).astype(jnp.bfloat16)
    hidden_out = mixed + product(activated, w_down)
    stored = (
        inverse_one,
        normed_one,
        normed_in,
        queries,
        key_rot,
        value_proj,
        logsum,
        context,
        inverse_two,
        normed_two,
        normed_mid,
        gate_pre,
        up_proj,
        activated,
        key_mask,
        cosine_table,
        sine_table,
    )
    return (hidden_out, stored)


def mlp_backward(stored, grad_out, mlp_gain, w_gate, w_up, w_down):
    inverse_two, normed_two, normed_mid, gate_pre, up_proj, activated = stored[8:14]
    grad_low = grad_out.astype(jnp.bfloat16)
    grad_act = product(grad_low, w_down.T)
    gate_sigmoid = jax.nn.sigmoid(gate_pre)
    grad_gate_pre = (
        grad_act * up_proj * gate_sigmoid * (1.0 + gate_pre * (1.0 - gate_sigmoid))
    ).astype(jnp.bfloat16)
    grad_up_pre = (grad_act * gate_pre * gate_sigmoid).astype(jnp.bfloat16)
    grad_mid = product(grad_gate_pre, w_gate.T) + product(grad_up_pre, w_up.T)
    grad_mlp_gain = jnp.sum(grad_mid * normed_two, axis=0)
    grad_mixed = grad_out + rms_back(grad_mid * mlp_gain, normed_two, inverse_two)
    pairs = ((normed_mid, grad_gate_pre), (normed_mid, grad_up_pre), (activated, grad_low))
    return (grad_mixed, grad_mlp_gain, pairs)


def attn_backward(stored, grad_mixed, attn_gain, w_query, w_key, w_value, w_output):
    inverse_one, normed_one, normed_in, queries, key_rot, value_proj, logsum, context = stored[:8]
    key_mask, cosine_table, sine_table = stored[14:17]
    groups, row_count, kv_count, repeat, _ = queries.shape
    head_count = kv_count * repeat
    score_scale = 1.0 / math.sqrt(HEAD_DIM)
    grad_low = grad_mixed.astype(jnp.bfloat16)
    grad_context = product(grad_low, w_output.T).astype(jnp.bfloat16)
    grad_context = grad_context.reshape(groups, row_count, kv_count, repeat, HEAD_DIM)
    scores = masked_scores(queries, key_rot, key_mask)
    attn_probs = jnp.exp(scores - logsum)
    probs_low = attn_probs.astype(jnp.bfloat16)
    grad_probs = batched("gqkrd,gskd->gkrqs", grad_context, value_proj)
    context_heads = context.reshape(groups, row_count, kv_count, repeat, HEAD_DIM)
    row_dot = jnp.sum(grad_context.astype(jnp.float32) * context_heads.astype(jnp.float32), axis=-1)
    row_dot = jnp.transpose(row_dot, (0, 2, 3, 1))[..., None]
    grad_scores = (attn_probs * (grad_probs - row_dot) * score_scale).astype(jnp.bfloat16)
    grad_values = batched("gkrqs,gqkrd->gskd", probs_low, grad_context).astype(jnp.bfloat16)
    grad_values = grad_values.reshape(groups * row_count, kv_count * HEAD_DIM)
    grad_queries = batched("gkrqs,gskd->gqkrd", grad_scores, key_rot).reshape(
        groups, row_count, head_count, HEAD_DIM
    )
    grad_queries = rotate_back(grad_queries, cosine_table, sine_table).astype(jnp.bfloat16)
    grad_queries = grad_queries.reshape(groups * row_count, head_count * HEAD_DIM)
    grad_keys = batched("gkrqs,gqkrd->gskd", grad_scores, queries)
    grad_keys = rotate_back(grad_keys, cosine_table, sine_table).astype(jnp.bfloat16)
    grad_keys = grad_keys.reshape(groups * row_count, kv_count * HEAD_DIM)
    grad_normed = (
        product(grad_queries, w_query.T)
        + product(grad_keys, w_key.T)
        + product(grad_values, w_value.T)
    )
    grad_attn_gain = jnp.sum(grad_normed * normed_one, axis=0)
    grad_in = grad_mixed + rms_back(grad_normed * attn_gain, normed_one, inverse_one)
    pairs = (
        (normed_in, grad_queries),
        (normed_in, grad_keys),
        (normed_in, grad_values),
        (context, grad_low),
    )
    return (grad_in, grad_attn_gain, pairs)


def flat_rows(left, right):
    block = lax.dot_general(
        left, right, (((0,), (0,)), ((), ())), preferred_element_type=jnp.float32
    )
    return block.reshape(-1)


def grad_term(pairs, shard_sizes):
    per_device = sum(shard_sizes)

    def term(start, count):
        owners = count // per_device
        pieces = [
            flat_rows(left, right).reshape(owners, size)
            for (left, right), size in zip(pairs, shard_sizes)
        ]
        return jnp.concatenate(pieces, axis=1).reshape(-1)

    return (term, per_device)


def split_shards(summed, shard_sizes):
    pieces = []
    offset = 0
    for size in shard_sizes:
        pieces.append(summed[offset : offset + size])
        offset = offset + size
    return tuple(pieces)


def shape_attn(flat_parts):
    query_width = HEADS * HEAD_DIM
    kv_width = KV_HEADS * HEAD_DIM
    return (
        flat_parts[0].reshape(D, query_width),
        flat_parts[1].reshape(D, kv_width),
        flat_parts[2].reshape(D, kv_width),
        flat_parts[3].reshape(query_width, D),
    )


def shape_mlp(flat_parts):
    return (
        flat_parts[0].reshape(D, FF),
        flat_parts[1].reshape(D, FF),
        flat_parts[2].reshape(FF, D),
    )


def plain_shards(
    hidden_in,
    seq_lens,
    attn_gain,
    w_query,
    w_key,
    w_value,
    w_output,
    mlp_gain,
    w_gate,
    w_up,
    w_down,
    grad_out,
):
    attn_sizes = (w_query.shape[0], w_key.shape[0], w_value.shape[0], w_output.shape[0])
    mlp_sizes = (w_gate.shape[0], w_up.shape[0], w_down.shape[0])
    attn_mats = shape_attn(
        (
            lax.all_gather(w_query, "fsdp", axis=0, tiled=True),
            lax.all_gather(w_key, "fsdp", axis=0, tiled=True),
            lax.all_gather(w_value, "fsdp", axis=0, tiled=True),
            lax.all_gather(w_output, "fsdp", axis=0, tiled=True),
        )
    )
    mlp_mats = shape_mlp(
        (
            lax.all_gather(w_gate, "fsdp", axis=0, tiled=True),
            lax.all_gather(w_up, "fsdp", axis=0, tiled=True),
            lax.all_gather(w_down, "fsdp", axis=0, tiled=True),
        )
    )
    hidden_out, stored = forward_pass(
        hidden_in,
        seq_lens,
        attn_gain,
        attn_mats[0],
        attn_mats[1],
        attn_mats[2],
        attn_mats[3],
        mlp_gain,
        mlp_mats[0],
        mlp_mats[1],
        mlp_mats[2],
    )
    mlp_back = shape_mlp(
        (
            lax.all_gather(w_gate, "fsdp", axis=0, tiled=True),
            lax.all_gather(w_up, "fsdp", axis=0, tiled=True),
            lax.all_gather(w_down, "fsdp", axis=0, tiled=True),
        )
    )
    grad_mixed, grad_mg, mlp_pairs = mlp_backward(
        stored, grad_out, mlp_gain, mlp_back[0], mlp_back[1], mlp_back[2]
    )
    mlp_fn, mlp_rows = grad_term(mlp_pairs, mlp_sizes)
    mlp_shards = split_shards(
        lax.psum_scatter(
            mlp_fn(jnp.int32(0), lax.axis_size("fsdp") * mlp_rows),
            "fsdp",
            scatter_dimension=0,
            tiled=True,
        ),
        mlp_sizes,
    )
    attn_back = shape_attn(
        (
            lax.all_gather(w_query, "fsdp", axis=0, tiled=True),
            lax.all_gather(w_key, "fsdp", axis=0, tiled=True),
            lax.all_gather(w_value, "fsdp", axis=0, tiled=True),
            lax.all_gather(w_output, "fsdp", axis=0, tiled=True),
        )
    )
    grad_in, grad_ag, attn_pairs = attn_backward(
        stored, grad_mixed, attn_gain, attn_back[0], attn_back[1], attn_back[2], attn_back[3]
    )
    attn_fn, attn_rows = grad_term(attn_pairs, attn_sizes)
    attn_shards = split_shards(
        lax.psum_scatter(
            attn_fn(jnp.int32(0), lax.axis_size("fsdp") * attn_rows),
            "fsdp",
            scatter_dimension=0,
            tiled=True,
        ),
        attn_sizes,
    )
    weight_shards = attn_shards + mlp_shards
    gain_totals = lax.psum((grad_ag, grad_mg), "fsdp")
    return (
        hidden_out,
        grad_in,
        gain_totals[0],
        gain_totals[1],
        weight_shards[0],
        weight_shards[1],
        weight_shards[2],
        weight_shards[3],
        weight_shards[4],
        weight_shards[5],
        weight_shards[6],
    )


def solution(mesh):
    placed = (
        P("fsdp", None),
        P("fsdp", None),
        P(),
        P("fsdp"),
        P("fsdp"),
        P("fsdp"),
        P("fsdp"),
        P(),
        P("fsdp"),
        P("fsdp"),
        P("fsdp"),
        P("fsdp", None),
    )
    count = mesh.shape[AXIS]
    whole_rows = D % count == 0 and FF % count == 0 and count in (2 * GROUP, 4 * GROUP)
    return jax.shard_map(
        shards if whole_rows else plain_shards,
        mesh=mesh,
        in_specs=placed,
        out_specs=(
            P("fsdp", None),
            P("fsdp", None),
            P(),
            P(),
            P("fsdp"),
            P("fsdp"),
            P("fsdp"),
            P("fsdp"),
            P("fsdp"),
            P("fsdp"),
            P("fsdp"),
        ),
        check_vma=False,
    )
```

```python
import math

import jax
import jax.numpy as jnp
from jax import lax
from jax.experimental import pallas as pl
from jax.experimental.pallas import tpu as pltpu
from jax.sharding import PartitionSpec as P


D = 960
HEADS = 15
KV_HEADS = 5
HEAD_DIM = 64
FF = 2560


EPS = 1e-05
ROPE_BASE = 100000.0
AXIS = "fsdp"
GROUP = 8
SUBLANES = 16
LANES = 128
LOW = jnp.bfloat16


def product(left, right):
    return jnp.dot(left, right, preferred_element_type=jnp.float32)


def product_t(left, right):
    return lax.dot_general(left, right, (((1,), (1,)), ((), ())), preferred_element_type=jnp.float32)


def t_product(left, right):
    return lax.dot_general(left, right, (((0,), (0,)), ((), ())), preferred_element_type=jnp.float32)


def batched(form, left, right):
    return jnp.einsum(form, left, right, preferred_element_type=jnp.float32)


def rms_scale(values):
    inverse = lax.rsqrt(jnp.mean(values * values, axis=-1, keepdims=True) + EPS)
    return (inverse, values * inverse)


def rms_back(grad_normed, normed, inverse):
    return inverse * (grad_normed - normed * jnp.mean(grad_normed * normed, axis=-1, keepdims=True))


def seq_layout(lengths, row_count):
    ends = jnp.cumsum(lengths, axis=1)
    row_index = jnp.arange(row_count, dtype=jnp.int32)
    after = (row_index[None, :, None] >= ends[:, None, :]).astype(jnp.int32)
    segment = jnp.sum(after, axis=2)
    starts = jnp.sum(after * lengths[:, None, :], axis=2)
    return (segment, row_index[None, :] - starts)


def rotary_tables(position):
    half_dim = HEAD_DIM // 2
    freqs = ROPE_BASE ** (-(jnp.arange(half_dim, dtype=jnp.float32) * 2.0) / HEAD_DIM)
    angles = position.astype(jnp.float32)[:, :, None] * freqs[None, None, :]
    return (jnp.cos(angles)[:, :, None, :], jnp.sin(angles)[:, :, None, :])


def rotate(vectors, cosine_table, sine_table):
    half_dim = HEAD_DIM // 2
    first, second = (vectors[..., :half_dim], vectors[..., half_dim:])
    return jnp.concatenate(
        [first * cosine_table - second * sine_table, second * cosine_table + first * sine_table],
        axis=-1,
    )


def rotate_back(vectors, cosine_table, sine_table):
    return rotate(vectors, cosine_table, -sine_table)


def masked_scores(queries, key_rot, key_mask):
    score_scale = 1.0 / math.sqrt(HEAD_DIM)
    scores = batched("gqkrd,gskd->gkrqs", queries, key_rot) * score_scale
    return jnp.where(key_mask[:, None, None, :, :], scores, -1e30)


def attn_core(qkv, lengths):
    groups = lengths.shape[0]
    rows = qkv.shape[0] // groups
    repeat = HEADS // KV_HEADS
    segment, position = seq_layout(lengths, rows)
    cosine, sine = rotary_tables(position)
    causal = jnp.arange(rows)[:, None] >= jnp.arange(rows)[None, :]
    key_mask = (segment[:, :, None] == segment[:, None, :]) & causal[None, :, :]
    q_width, kv_width = HEADS * HEAD_DIM, KV_HEADS * HEAD_DIM
    query = qkv[:, :q_width].reshape(groups, rows, HEADS, HEAD_DIM)
    key = qkv[:, q_width : q_width + kv_width].reshape(groups, rows, KV_HEADS, HEAD_DIM)
    queries = rotate(query, cosine, sine).astype(LOW).reshape(groups, rows, KV_HEADS, repeat, HEAD_DIM)
    key_rot = rotate(key, cosine, sine).astype(LOW)
    values = qkv[:, q_width + kv_width :].astype(LOW).reshape(groups, rows, KV_HEADS, HEAD_DIM)
    scores = masked_scores(queries, key_rot, key_mask)
    peak = jnp.max(scores, axis=-1, keepdims=True)
    logsum = peak + jnp.log(jnp.sum(jnp.exp(scores - peak), axis=-1, keepdims=True))
    probs = jnp.exp(scores - logsum).astype(LOW)
    context = batched("gkrqs,gskd->gqkrd", probs, values).astype(LOW)
    context = context.reshape(groups * rows, q_width)
    return context, (queries, key_rot, values, logsum, context, key_mask, cosine, sine)


def attn_core_back(stored, grad_context):
    queries, key_rot, values, logsum, context, key_mask, cosine, sine = stored
    groups, rows, kv_count, repeat, _ = queries.shape
    score_scale = 1.0 / math.sqrt(HEAD_DIM)
    grad_context = grad_context.reshape(groups, rows, kv_count, repeat, HEAD_DIM)
    probs = jnp.exp(masked_scores(queries, key_rot, key_mask) - logsum)
    grad_probs = batched("gqkrd,gskd->gkrqs", grad_context, values)
    heads = context.reshape(groups, rows, kv_count, repeat, HEAD_DIM)
    row_dot = jnp.sum(grad_context.astype(jnp.float32) * heads.astype(jnp.float32), axis=-1)
    row_dot = jnp.transpose(row_dot, (0, 2, 3, 1))[..., None]
    grad_scores = (probs * (grad_probs - row_dot) * score_scale).astype(LOW)
    grad_values = batched("gkrqs,gqkrd->gskd", probs.astype(LOW), grad_context).astype(LOW)
    grad_queries = batched("gkrqs,gskd->gqkrd", grad_scores, key_rot)
    grad_queries = grad_queries.reshape(groups, rows, HEADS, HEAD_DIM)
    grad_queries = rotate_back(grad_queries, cosine, sine).astype(LOW)
    grad_keys = batched("gkrqs,gqkrd->gskd", grad_scores, queries)
    grad_keys = rotate_back(grad_keys, cosine, sine).astype(LOW)
    flat = groups * rows
    return jnp.concatenate(
        [grad_queries.reshape(flat, -1), grad_keys.reshape(flat, -1), grad_values.reshape(flat, -1)],
        axis=1,
    )


def sum_all(total, terms):
    for term in terms:
        total = total + term.astype(jnp.float32)
    return total


def part_tables(pieces, spots, width):
    count, (rows, columns) = len(pieces), pieces[0].shape
    depth, rest = rows // 3, columns - width

    def kernel(table_ref, *refs):
        left_ref, right_ref = refs[count:]
        for k in range(count):
            at = table_ref[k]
            left_ref[at] = refs[k][:, :width]
            for j in range(3):
                third = refs[k][depth * j : depth * (j + 1), width:]
                right_ref[at, :, rest * j : rest * (j + 1)] = third

    here = pl.BlockSpec(memory_space=pltpu.VMEM)
    return pl.pallas_call(
        kernel,
        out_shape=[
            jax.ShapeDtypeStruct((count, rows, width), pieces[0].dtype),
            jax.ShapeDtypeStruct((count, depth, 3 * rest), pieces[0].dtype),
        ],
        in_specs=[pl.BlockSpec(memory_space=pltpu.SMEM)] + [here] * count,
        out_specs=[here, here],
        name="part_tables",
    )(jnp.stack(spots).astype(jnp.int32), *pieces)


def spread_columns(blocks, planes, depth):
    rows = blocks.shape[1]

    def kernel(blocks_ref, *targets):
        for b in range(GROUP):
            block = blocks_ref[b].astype(jnp.float32)
            for t, target in enumerate(targets):
                for p in range(planes):
                    start, to = (t * planes + p) * depth, (p * GROUP + b) * depth
                    target[:, to : to + depth] = block[:, start : start + depth]

    here = pl.BlockSpec(memory_space=pltpu.VMEM)
    shape = jax.ShapeDtypeStruct((rows, planes * GROUP * depth), jnp.float32)
    return pl.pallas_call(
        kernel, out_shape=[shape, shape], in_specs=[here], out_specs=[here, here], name="spread_columns"
    )(blocks)


def weight_terms(pairs, starts, width, dtype):
    rows = pairs[0][0].shape[1]

    def kernel(*refs):
        target = refs[-1]
        for k, start in enumerate(starts):
            left, right = refs[2 * k][...], refs[2 * k + 1][...]
            stop = start + right.shape[0]
            term = lax.dot_general(left, right, (((0,), (1,)), ((), ())), preferred_element_type=jnp.float32)
            target[:, start:stop] = term.astype(dtype)
            gap = (starts + [width])[k + 1] - stop
            if gap:
                target[:, stop : stop + gap] = jnp.zeros((rows, gap), dtype)

    here = pl.BlockSpec(memory_space=pltpu.VMEM)
    return pl.pallas_call(
        kernel,
        out_shape=jax.ShapeDtypeStruct((rows, width), dtype),
        in_specs=[here] * (2 * len(pairs)),
        out_specs=here,
        name="weight_terms",
    )(*[array for pair in pairs for array in pair])


class Links:
    def __init__(self, count):
        self.count = count
        self.planes = count // GROUP
        self.me = lax.axis_index(AXIS)
        self.plane = self.me // GROUP
        self.quads = [[p * GROUP + 2 * k + c for k in range(4)] for p in range(self.planes) for c in range(2)]
        self.groups = [[p * GROUP + k for k in range(GROUP)] for p in range(self.planes)]

    def flip(self, value, bit):
        return lax.ppermute(value, AXIS, [(i, i ^ bit) for i in range(self.count)])

    def shift(self, value, step):
        return lax.ppermute(value, AXIS, [(i, (i + step * GROUP) % self.count) for i in range(self.count)])

    def behind(self, step):
        return (self.plane - step) % self.planes

    def device_at(self, place_index):
        step = place_index % self.planes
        chip = place_index // self.planes % 4
        bits = chip % 2 * 2 + chip // 2 * 4 + place_index // (4 * self.planes)
        spot = self.me % GROUP
        flipped = jnp.where(bits & 1, spot ^ 1, spot)
        flipped = jnp.where(bits & 2, flipped ^ 2, flipped)
        flipped = jnp.where(bits & 4, flipped ^ 4, flipped)
        return (self.plane - step) % self.planes * GROUP + flipped

    def gather_planes(self, block):
        pieces = [block] + [self.shift(block, step) for step in range(1, self.planes)]
        return pieces, [self.behind(step) for step in range(self.planes)]

    def send_planes(self, block_of):
        blocks = [block_of((self.plane + step) % self.planes).astype(LOW) for step in range(1, self.planes)]
        return [self.shift(block, step + 1) for step, block in enumerate(blocks)]

    def gather_behind(self, block):
        return jnp.stack([block] + [self.shift(block, step) for step in range(1, self.planes)])

    def scatter_behind(self, rows, late):
        blocks = [rows[step].astype(LOW) for step in range(1, self.planes)]
        blocks, late = lax.optimization_barrier((blocks, late))
        terms = [self.shift(block, -1 - step) for step, block in enumerate(blocks)]
        return sum_all(rows[0], terms), late

    def gather_rows(self, own):
        half = self.planes // 2
        by_x, by_y = self.flip(own, 2), self.flip(own, 4)
        pieces = [own, by_x, by_y, self.flip(by_x[:half], 4), self.flip(by_y[half:], 2)]
        others = [self.flip(piece, 1) for piece in pieces]
        rows = (4 * self.planes * own.shape[1], own.shape[2])
        return jnp.concatenate(pieces).reshape(rows), jnp.concatenate(others).reshape(rows)

    def scatter_quad(self, terms, cut, early=(), late=()):
        def part(chip, half):
            return cut(terms[0], chip, half) + cut(terms[1], chip, half).astype(jnp.float32)

        corner = [part(3, half).astype(LOW) for half in range(2)]
        corner, early, terms = lax.optimization_barrier((corner, early, terms))
        by_y, by_x = self.flip(corner[0], 4), self.flip(corner[1], 2)
        by_y, by_x = by_y.astype(jnp.float32), by_x.astype(jnp.float32)
        to_x = jnp.stack([(part(1, 0) + by_y).astype(LOW), part(1, 1).astype(LOW)])
        to_y = jnp.stack([part(2, 0).astype(LOW), (part(2, 1) + by_x).astype(LOW)])
        to_x, to_y, late, terms = lax.optimization_barrier((to_x, to_y, late, terms))
        from_x, from_y = self.flip(to_x, 2), self.flip(to_y, 4)
        return [sum_all(part(0, half), [from_x[half], from_y[half]]) for half in range(2)], early, late

    def with_other(self, own, away):
        return own, self.flip(away, 1)

    def blocks(self, rows):
        return rows.reshape(4 * self.planes, rows.shape[0] // (4 * self.planes), rows.shape[1])

    def scatter_rows(self, terms, early, late):
        half = self.planes // 2

        def cut(term, chip, side):
            start = (2 * chip + side) * half
            return term[start : start + half]

        halves, early, late = self.scatter_quad(terms, cut, early, late)
        return jnp.concatenate(halves), early, late

    def gather_tokens(self, block):
        quad = lax.all_gather(block, AXIS, axis=0, tiled=True, axis_index_groups=self.quads)
        return quad, self.flip(quad, 1)

    def gather_aside(self, block):
        (count, width), spot = block.shape, self.me % GROUP // 2
        half = width // 2
        by_x, by_y = self.flip(block, 2), self.flip(block, 4)
        corner_y, corner_x = self.flip(by_x[:, :half], 4), self.flip(by_y[:, half:], 2)
        quad = jnp.zeros((4 * count, width), block.dtype)
        for chip, column, value in ((0, 0, block), (1, 0, by_x), (2, 0, by_y), (3, 0, corner_y), (3, half, corner_x)):
            quad = lax.dynamic_update_slice(quad, value, ((spot ^ chip) * count, column))
        return quad, self.flip(quad, 1)

    def scatter_tokens(self, terms, early=()):
        (rows, width), spot = terms[0].shape, self.me % GROUP // 2
        count, width = rows // 4, width // 2

        def cut(term, chip, side):
            return lax.dynamic_slice(term, ((spot ^ chip) * count, side * width), (count, width))

        halves, early, _ = self.scatter_quad(terms, cut, early)
        return jnp.concatenate(halves, axis=1), early

    def swap(self, blocks):
        return lax.all_to_all(
            blocks, AXIS, split_axis=0, concat_axis=0, tiled=True, axis_index_groups=self.groups
        )

    def add_over(self, values, bits):
        for bit in bits:
            values = values + self.flip(values, bit)
        return values


def padded(depth):
    return -(-depth // SUBLANES) * SUBLANES


def spread_matrix(links, depth):
    wide = padded(depth)
    column = lax.broadcasted_iota(jnp.int32, (1, links.count * wide), 1)
    inside = column % wide
    source = jnp.where(inside < depth, links.device_at(column // wide) * depth + inside, -1)
    row = lax.broadcasted_iota(jnp.int32, (links.count * depth, links.count * wide), 0)
    return (row == source).astype(LOW)


def pad_rows(block):
    return jnp.pad(block, ((0, padded(block.shape[0]) - block.shape[0]), (0, 0)))


def narrow(values, spread):
    high = lax.reduce_precision(values, 8, 7)
    low = (values - high).astype(LOW)
    return product_t(high.astype(LOW), spread) + product_t(low, spread)


def shards(*args):
    return layer(*args)


def layer(
    hidden_in, seq_lens, attn_gain, w_query, w_key, w_value, w_output, mlp_gain, w_gate, w_up, w_down, grad_out
):
    count = lax.axis_size(AXIS)
    links = Links(count)
    planes = links.planes
    depth, ff_depth = D // count, FF // count
    q_width, kv_width = HEADS * HEAD_DIM, KV_HEADS * HEAD_DIM
    slice_width = planes * ff_depth
    spread = spread_matrix(links, depth)

    qkv_width = q_width + 2 * kv_width
    lanes = -(-qkv_width // LANES) * LANES
    attn_block = jnp.concatenate(
        [
            w_query.reshape(depth, q_width),
            w_key.reshape(depth, kv_width),
            w_value.reshape(depth, kv_width),
            jnp.zeros((depth, lanes - qkv_width), LOW),
            w_output.reshape(depth, D),
        ],
        axis=1,
    )
    attn_planes = links.gather_behind(pad_rows(attn_block))
    pair = jnp.stack([w_gate.reshape(depth, FF), w_up.reshape(depth, FF)])
    pair = pair.reshape(2, depth, planes, GROUP, ff_depth)
    pair = jnp.transpose(pair, (3, 1, 0, 2, 4)).reshape(GROUP, depth, 2 * slice_width)
    pair, grad_early = lax.optimization_barrier((pair, grad_out))
    pair = links.swap(pair).reshape(GROUP * depth, 2 * slice_width)
    grad_early = grad_early.astype(LOW)
    grads = links.gather_aside(grad_early)
    attn_planes, w_down = lax.optimization_barrier((attn_planes, w_down))
    tables = links.gather_rows(attn_planes)
    w_qkv = [table[:, :qkv_width] for table in tables]
    w_out = [table[:, lanes:] for table in tables]
    mine = tables[0].shape[0]
    thirds = jnp.concatenate(jnp.split(w_down.reshape(ff_depth, D), 3, axis=1))
    ff_pieces, ff_spots = links.gather_planes(jnp.concatenate([pair, thirds], axis=1))

    inverse_one, normed_one = rms_scale(hidden_in)
    normed_in = (normed_one * attn_gain).astype(LOW)
    spread_in = product(normed_in, spread).astype(LOW)
    qkv = product(spread_in[:, :mine], w_qkv[0]) + product(spread_in[:, mine:], w_qkv[1])
    context, stored = attn_core(qkv, seq_lens)
    spread_context = product(context, spread).astype(LOW)
    mixed = hidden_in + (
        product(spread_context[:, :mine], w_out[0]) + product(spread_context[:, mine:], w_out[1])
    )

    inverse_two, normed_two = rms_scale(mixed)
    normed_mid = (normed_two * mlp_gain).astype(LOW)
    w_pair, w_back = part_tables(ff_pieces, ff_spots, 2 * slice_width)
    w_pair, w_back = w_pair.reshape(D, 2 * slice_width), w_back.reshape(slice_width, D)
    tokens = links.gather_tokens(normed_mid)

    def unit(tokens, grads):
        both = product(tokens, w_pair)
        gate, up = both[:, :slice_width], both[:, slice_width:]
        sigmoid = jax.nn.sigmoid(gate)
        activated = (gate * sigmoid * up).astype(LOW)
        grad_act = product_t(grads, w_back)
        grad_gate = (grad_act * up * sigmoid * (1.0 + gate * (1.0 - sigmoid))).astype(LOW)
        grad_up = (grad_act * gate * sigmoid).astype(LOW)
        grad_both = jnp.concatenate([grad_gate, grad_up], axis=1)
        return activated, grad_both, product_t(grad_both, w_pair)

    far_active, far_both, mid_away = unit(tokens[1], grads[1])
    near_active, near_both, mid_own = unit(tokens[0], grads[0])
    grad_mid, early = links.scatter_tokens(
        links.with_other(mid_own, mid_away.astype(LOW)), (near_both, far_both, near_active, far_active)
    )
    near_both, far_both, near_active, far_active = early
    pair_term = (t_product(tokens[0], near_both) + t_product(tokens[1], far_both)).astype(LOW)
    pair_term = pair_term.reshape(planes, GROUP * depth, 2 * slice_width)
    down_term = (t_product(near_active, grads[0]) + t_product(far_active, grads[1])).astype(LOW)
    down_term = down_term.reshape(planes, ff_depth, D)

    def ff_block(p):
        down = lax.dynamic_index_in_dim(down_term, p, 0, keepdims=False)
        thirds = jnp.concatenate(jnp.split(down, 3, axis=1))
        return jnp.concatenate([lax.dynamic_index_in_dim(pair_term, p, 0, keepdims=False), thirds], axis=1)

    ff_own, ff_terms = ff_block(links.plane), links.send_planes(ff_block)
    grad_mlp_gain = jnp.sum(grad_mid * normed_two, axis=0)
    grad_mixed = grad_out + rms_back(grad_mid * mlp_gain, normed_two, inverse_two)

    grad_low = grad_mixed.astype(LOW)
    grad_context = jnp.concatenate([product_t(grad_low, part).astype(LOW) for part in w_out], axis=1)
    grad_context = product_t(grad_context, spread).astype(LOW)
    grad_qkv = attn_core_back(stored, grad_context)
    far_term, near_term = [
        weight_terms(
            [(spread_in[:, side], grad_qkv.T), (spread_context[:, side], grad_low.T)],
            [0, lanes],
            lanes + D,
            dtype,
        )
        for side, dtype in ((slice(mine, None), LOW), (slice(0, mine), jnp.float32))
    ]
    attn_sums = links.with_other(links.blocks(near_term), links.blocks(far_term))

    late = (near_active, far_active, ff_own, ff_terms)
    attn_sums, late_qkv, late = links.scatter_rows(attn_sums, grad_qkv, late)
    near_active, far_active, ff_own, ff_terms = late
    grad_normed = jnp.concatenate([product_t(late_qkv, part) for part in w_qkv], axis=1)
    grad_normed = narrow(grad_normed, spread)
    grad_attn_gain = jnp.sum(grad_normed * normed_one, axis=0)
    grad_in = grad_mixed + rms_back(grad_normed * attn_gain, normed_one, inverse_one)
    plane_bits = [GROUP << k for k in range(planes.bit_length() - 1)]
    gains = links.add_over(jnp.stack([grad_attn_gain, grad_mlp_gain]), plane_bits + [1])
    hidden_sums = links.with_other(product(near_active, w_back), product(far_active, w_back).astype(LOW))
    ff_sum = sum_all(ff_own.astype(jnp.float32), ff_terms)
    pair_sum, down_sum = ff_sum[:, : 2 * slice_width], ff_sum[:, 2 * slice_width :]
    down_sum = jnp.concatenate(jnp.split(down_sum, 3), axis=1)
    pair_sum = pair_sum.astype(LOW).reshape(GROUP, depth, 2 * slice_width)
    attn_sum, (pair_sum, gains) = links.scatter_behind(attn_sums, (pair_sum, gains))
    gains = links.add_over(gains, [2, 4])
    attn_sum = attn_sum[:depth]
    qkv_sum, out_sum = attn_sum[:, :qkv_width], attn_sum[:, lanes:]
    pair_sum = links.swap(pair_sum)
    gate_sum, up_sum = spread_columns(pair_sum, planes, ff_depth)
    hidden_out = mixed + links.scatter_tokens(hidden_sums)[0]
    return (
        hidden_out,
        grad_in,
        gains[0],
        gains[1],
        qkv_sum[:, :q_width].reshape(-1),
        qkv_sum[:, q_width : q_width + kv_width].reshape(-1),
        qkv_sum[:, q_width + kv_width :].reshape(-1),
        out_sum.reshape(-1),
        gate_sum.reshape(-1),
        up_sum.reshape(-1),
        down_sum.reshape(-1),
    )


def forward_pass(
    hidden_in, lengths, attn_gain, w_query, w_key, w_value, w_output, mlp_gain, w_gate, w_up, w_down
):
    groups = lengths.shape[0]
    row_count = hidden_in.shape[0] // groups
    head_count = w_query.shape[1] // HEAD_DIM
    kv_count = w_key.shape[1] // HEAD_DIM
    repeat = head_count // kv_count
    segment, position = seq_layout(lengths, row_count)
    cosine_table, sine_table = rotary_tables(position)
    causal = jnp.arange(row_count)[:, None] >= jnp.arange(row_count)[None, :]
    key_mask = (segment[:, :, None] == segment[:, None, :]) & causal[None, :, :]
    inverse_one, normed_one = rms_scale(hidden_in)
    normed_in = (normed_one * attn_gain).astype(jnp.bfloat16)
    query_proj = product(normed_in, w_query).reshape(groups, row_count, head_count, HEAD_DIM)
    queries = rotate(query_proj, cosine_table, sine_table).astype(jnp.bfloat16)
    queries = queries.reshape(groups, row_count, kv_count, repeat, HEAD_DIM)
    key_proj = product(normed_in, w_key).reshape(groups, row_count, kv_count, HEAD_DIM)
    key_rot = rotate(key_proj, cosine_table, sine_table).astype(jnp.bfloat16)
    value_proj = (
        product(normed_in, w_value)
        .astype(jnp.bfloat16)
        .reshape(groups, row_count, kv_count, HEAD_DIM)
    )
    scores = masked_scores(queries, key_rot, key_mask)
    row_peak = jnp.max(scores, axis=-1, keepdims=True)
    row_total = jnp.sum(jnp.exp(scores - row_peak), axis=-1, keepdims=True)
    logsum = row_peak + jnp.log(row_total)
    attn_probs = jnp.exp(scores - logsum).astype(jnp.bfloat16)
    context = batched("gkrqs,gskd->gqkrd", attn_probs, value_proj).astype(jnp.bfloat16)
    context = context.reshape(groups * row_count, head_count * HEAD_DIM)
    mixed = hidden_in + product(context, w_output)
    inverse_two, normed_two = rms_scale(mixed)
    normed_mid = (normed_two * mlp_gain).astype(jnp.bfloat16)
    gate_pre = product(normed_mid, w_gate)
    up_proj = product(normed_mid, w_up)
    gate_sigmoid = jax.nn.sigmoid(gate_pre)
    activated = (gate_pre * gate_sigmoid * up_proj).astype(jnp.bfloat16)
    hidden_out = mixed + product(activated, w_down)
    stored = (
        inverse_one,
        normed_one,
        normed_in,
        queries,
        key_rot,
        value_proj,
        logsum,
        context,
        inverse_two,
        normed_two,
        normed_mid,
        gate_pre,
        up_proj,
        activated,
        key_mask,
        cosine_table,
        sine_table,
    )
    return (hidden_out, stored)


def mlp_backward(stored, grad_out, mlp_gain, w_gate, w_up, w_down):
    inverse_two, normed_two, normed_mid, gate_pre, up_proj, activated = stored[8:14]
    grad_low = grad_out.astype(jnp.bfloat16)
    grad_act = product(grad_low, w_down.T)
    gate_sigmoid = jax.nn.sigmoid(gate_pre)
    grad_gate_pre = (
        grad_act * up_proj * gate_sigmoid * (1.0 + gate_pre * (1.0 - gate_sigmoid))
    ).astype(jnp.bfloat16)
    grad_up_pre = (grad_act * gate_pre * gate_sigmoid).astype(jnp.bfloat16)
    grad_mid = product(grad_gate_pre, w_gate.T) + product(grad_up_pre, w_up.T)
    grad_mlp_gain = jnp.sum(grad_mid * normed_two, axis=0)
    grad_mixed = grad_out + rms_back(grad_mid * mlp_gain, normed_two, inverse_two)
    pairs = ((normed_mid, grad_gate_pre), (normed_mid, grad_up_pre), (activated, grad_low))
    return (grad_mixed, grad_mlp_gain, pairs)


def attn_backward(stored, grad_mixed, attn_gain, w_query, w_key, w_value, w_output):
    inverse_one, normed_one, normed_in, queries, key_rot, value_proj, logsum, context = stored[:8]
    key_mask, cosine_table, sine_table = stored[14:17]
    groups, row_count, kv_count, repeat, _ = queries.shape
    head_count = kv_count * repeat
    score_scale = 1.0 / math.sqrt(HEAD_DIM)
    grad_low = grad_mixed.astype(jnp.bfloat16)
    grad_context = product(grad_low, w_output.T).astype(jnp.bfloat16)
    grad_context = grad_context.reshape(groups, row_count, kv_count, repeat, HEAD_DIM)
    scores = masked_scores(queries, key_rot, key_mask)
    attn_probs = jnp.exp(scores - logsum)
    probs_low = attn_probs.astype(jnp.bfloat16)
    grad_probs = batched("gqkrd,gskd->gkrqs", grad_context, value_proj)
    context_heads = context.reshape(groups, row_count, kv_count, repeat, HEAD_DIM)
    row_dot = jnp.sum(grad_context.astype(jnp.float32) * context_heads.astype(jnp.float32), axis=-1)
    row_dot = jnp.transpose(row_dot, (0, 2, 3, 1))[..., None]
    grad_scores = (attn_probs * (grad_probs - row_dot) * score_scale).astype(jnp.bfloat16)
    grad_values = batched("gkrqs,gqkrd->gskd", probs_low, grad_context).astype(jnp.bfloat16)
    grad_values = grad_values.reshape(groups * row_count, kv_count * HEAD_DIM)
    grad_queries = batched("gkrqs,gskd->gqkrd", grad_scores, key_rot).reshape(
        groups, row_count, head_count, HEAD_DIM
    )
    grad_queries = rotate_back(grad_queries, cosine_table, sine_table).astype(jnp.bfloat16)
    grad_queries = grad_queries.reshape(groups * row_count, head_count * HEAD_DIM)
    grad_keys = batched("gkrqs,gqkrd->gskd", grad_scores, queries)
    grad_keys = rotate_back(grad_keys, cosine_table, sine_table).astype(jnp.bfloat16)
    grad_keys = grad_keys.reshape(groups * row_count, kv_count * HEAD_DIM)
    grad_normed = (
        product(grad_queries, w_query.T)
        + product(grad_keys, w_key.T)
        + product(grad_values, w_value.T)
    )
    grad_attn_gain = jnp.sum(grad_normed * normed_one, axis=0)
    grad_in = grad_mixed + rms_back(grad_normed * attn_gain, normed_one, inverse_one)
    pairs = (
        (normed_in, grad_queries),
        (normed_in, grad_keys),
        (normed_in, grad_values),
        (context, grad_low),
    )
    return (grad_in, grad_attn_gain, pairs)


def flat_rows(left, right):
    block = lax.dot_general(
        left, right, (((0,), (0,)), ((), ())), preferred_element_type=jnp.float32
    )
    return block.reshape(-1)


def grad_term(pairs, shard_sizes):
    per_device = sum(shard_sizes)

    def term(start, count):
        owners = count // per_device
        pieces = [
            flat_rows(left, right).reshape(owners, size)
            for (left, right), size in zip(pairs, shard_sizes)
        ]
        return jnp.concatenate(pieces, axis=1).reshape(-1)

    return (term, per_device)


def split_shards(summed, shard_sizes):
    pieces = []
    offset = 0
    for size in shard_sizes:
        pieces.append(summed[offset : offset + size])
        offset = offset + size
    return tuple(pieces)


def shape_attn(flat_parts):
    query_width = HEADS * HEAD_DIM
    kv_width = KV_HEADS * HEAD_DIM
    return (
        flat_parts[0].reshape(D, query_width),
        flat_parts[1].reshape(D, kv_width),
        flat_parts[2].reshape(D, kv_width),
        flat_parts[3].reshape(query_width, D),
    )


def shape_mlp(flat_parts):
    return (
        flat_parts[0].reshape(D, FF),
        flat_parts[1].reshape(D, FF),
        flat_parts[2].reshape(FF, D),
    )


def plain_shards(
    hidden_in,
    seq_lens,
    attn_gain,
    w_query,
    w_key,
    w_value,
    w_output,
    mlp_gain,
    w_gate,
    w_up,
    w_down,
    grad_out,
):
    attn_sizes = (w_query.shape[0], w_key.shape[0], w_value.shape[0], w_output.shape[0])
    mlp_sizes = (w_gate.shape[0], w_up.shape[0], w_down.shape[0])
    attn_mats = shape_attn(
        (
            lax.all_gather(w_query, "fsdp", axis=0, tiled=True),
            lax.all_gather(w_key, "fsdp", axis=0, tiled=True),
            lax.all_gather(w_value, "fsdp", axis=0, tiled=True),
            lax.all_gather(w_output, "fsdp", axis=0, tiled=True),
        )
    )
    mlp_mats = shape_mlp(
        (
            lax.all_gather(w_gate, "fsdp", axis=0, tiled=True),
            lax.all_gather(w_up, "fsdp", axis=0, tiled=True),
            lax.all_gather(w_down, "fsdp", axis=0, tiled=True),
        )
    )
    hidden_out, stored = forward_pass(
        hidden_in,
        seq_lens,
        attn_gain,
        attn_mats[0],
        attn_mats[1],
        attn_mats[2],
        attn_mats[3],
        mlp_gain,
        mlp_mats[0],
        mlp_mats[1],
        mlp_mats[2],
    )
    mlp_back = shape_mlp(
        (
            lax.all_gather(w_gate, "fsdp", axis=0, tiled=True),
            lax.all_gather(w_up, "fsdp", axis=0, tiled=True),
            lax.all_gather(w_down, "fsdp", axis=0, tiled=True),
        )
    )
    grad_mixed, grad_mg, mlp_pairs = mlp_backward(
        stored, grad_out, mlp_gain, mlp_back[0], mlp_back[1], mlp_back[2]
    )
    mlp_fn, mlp_rows = grad_term(mlp_pairs, mlp_sizes)
    mlp_shards = split_shards(
        lax.psum_scatter(
            mlp_fn(jnp.int32(0), lax.axis_size("fsdp") * mlp_rows),
            "fsdp",
            scatter_dimension=0,
            tiled=True,
        ),
        mlp_sizes,
    )
    attn_back = shape_attn(
        (
            lax.all_gather(w_query, "fsdp", axis=0, tiled=True),
            lax.all_gather(w_key, "fsdp", axis=0, tiled=True),
            lax.all_gather(w_value, "fsdp", axis=0, tiled=True),
            lax.all_gather(w_output, "fsdp", axis=0, tiled=True),
        )
    )
    grad_in, grad_ag, attn_pairs = attn_backward(
        stored, grad_mixed, attn_gain, attn_back[0], attn_back[1], attn_back[2], attn_back[3]
    )
    attn_fn, attn_rows = grad_term(attn_pairs, attn_sizes)
    attn_shards = split_shards(
        lax.psum_scatter(
            attn_fn(jnp.int32(0), lax.axis_size("fsdp") * attn_rows),
            "fsdp",
            scatter_dimension=0,
            tiled=True,
        ),
        attn_sizes,
    )
    weight_shards = attn_shards + mlp_shards
    gain_totals = lax.psum((grad_ag, grad_mg), "fsdp")
    return (
        hidden_out,
        grad_in,
        gain_totals[0],
        gain_totals[1],
        weight_shards[0],
        weight_shards[1],
        weight_shards[2],
        weight_shards[3],
        weight_shards[4],
        weight_shards[5],
        weight_shards[6],
    )


def solution(mesh):
    placed = (
        P("fsdp", None),
        P("fsdp", None),
        P(),
        P("fsdp"),
        P("fsdp"),
        P("fsdp"),
        P("fsdp"),
        P(),
        P("fsdp"),
        P("fsdp"),
        P("fsdp"),
        P("fsdp", None),
    )
    count = mesh.shape[AXIS]
    whole_rows = D % count == 0 and FF % count == 0 and count in (2 * GROUP, 4 * GROUP)
    return jax.shard_map(
        shards if whole_rows else plain_shards,
        mesh=mesh,
        in_specs=placed,
        out_specs=(
            P("fsdp", None),
            P("fsdp", None),
            P(),
            P(),
            P("fsdp"),
            P("fsdp"),
            P("fsdp"),
            P("fsdp"),
            P("fsdp"),
            P("fsdp"),
            P("fsdp"),
        ),
        check_vma=False,
    )
```
